32 devices in a mesh: row: 1, col: 16 (over z, y, core), seg: 2 (over x).
Axes of the slice: x: 2, y: 2, z: 4, core: 2. Of those that a mesh axis runs over, the one named last changes fastest.
Arguments:
- traces: bfloat16 [8, 128, 1024], P('seg', ('row', 'col')), may hold values from -600 to 600, as said below
- valid: int32 [8, 128], P('seg', ('row', 'col')), may hold values 0 or 1
Outputs:
- correlation: float32 [33, 1, 128, 128], P(None, None, ('col', 'seg'), 'row')
The draws below stay inside these ranges and needn't reach their ends.
Inputs may be any that keep to these rules, and one draw needn't show every extreme that they name: `traces`: samples of a common wavefield delayed by up to 32 samples per station plus noise, scaled per station.
All inputs are finite; a program needn't handle non-finite values. No bound on the sum of `valid` on one device may be relied on, other than what follows from the above.
Results may differ from the reference program's by a relative error of at most 0.002.
Values may be sent and summed in bfloat16 or wider, within the bound.
No kernel may reach another device: no remote copies, remote signals or barrier semaphores. Data moves between devices by JAX's collectives and lax.ppermute only.
A program may use at most 64 MiB of HBM per device.

```python
import math
import jax
import jax.numpy as jnp
from jax import lax

L = 1024
MAXLAG = 16
SEGS = 8
STATIONS = 128
N_ROW = 1


def draw_traces(key, part):
    key_source, key_offset, key_amp, key_noise = jax.random.split(key, 4)
    source = jnp.clip(jax.random.normal(key_source, (SEGS, L + 2 * MAXLAG), jnp.float32), -8.0, 8.0)
    offsets = jax.random.randint(key_offset, (STATIONS,), 0, 2 * MAXLAG + 1)
    positions = jnp.arange(L)[None, :] + offsets[:, None]
    shifted = source[:, positions]
    amplitude = jnp.exp(jax.random.uniform(key_amp, (STATIONS,), jnp.float32, 0.0, math.log(10.0)))
    noise = jnp.clip(jax.random.normal(key_noise, (SEGS, STATIONS, L), jnp.float32), -8.0, 8.0)
    weight_common = 0.7
    values = amplitude[None, :, None] * (weight_common * shifted + noise)
    return values.astype(jnp.bfloat16)


def with_ends(result, own_key, smallest, top_value):
    spot = [jax.random.randint(jax.random.fold_in(own_key, axis), (), 0, length) for axis, length in enumerate(result.shape)]
    widest = result.shape.index(max(result.shape))
    neighbour = spot[:widest] + [(spot[widest] + 1) % result.shape[widest]] + spot[widest + 1:]
    return result.at[tuple(spot)].set(smallest).at[tuple(neighbour)].set(top_value)


def setup_inputs(seed: int = 0) -> dict:
    streams_of = jax.random.split(jax.random.key(seed), 3)
    return {
        "traces": draw_traces(jax.random.fold_in(streams_of[2], 71), 0),
        "valid": with_ends((jax.random.randint(streams_of[1], (SEGS, STATIONS), 0, 4) < 3).astype(jnp.int32), jax.random.fold_in(streams_of[1], 1), 0, 1),
    }


def make_tables():
    bins = jnp.arange(L // 2, dtype=jnp.int32)
    samples = jnp.arange(L, dtype=jnp.int32)
    product = samples[:, None] * bins[None, :] % L
    angle = 2.0 * math.pi / L * product.astype(jnp.float32)
    dft_table = jnp.concatenate([jnp.cos(angle), -jnp.sin(angle)], axis=1).astype(jnp.bfloat16)
    shifts = jnp.arange(2 * MAXLAG + 1, dtype=jnp.int32) - MAXLAG
    lag_prod = shifts[:, None] * bins[None, :] % L
    lag_angle = 2.0 * math.pi / L * lag_prod.astype(jnp.float32)
    return (dft_table, jnp.cos(lag_angle), jnp.sin(lag_angle))

def whiten(traces, valid, dft_table):
    half = L // 2
    flat = traces.reshape(-1, L)
    spectrum = jnp.dot(flat, dft_table, preferred_element_type=jnp.float32)
    spectrum = spectrum.reshape(traces.shape[0], traces.shape[1], L)
    real_part = spectrum[..., :half]
    imag_part = spectrum[..., half:]
    power = real_part * real_part + imag_part * imag_part
    level = lax.optimization_barrier(jnp.mean(power, axis=-1, keepdims=True))
    factor = lax.rsqrt(power + 0.1 * level + 1e-05) * valid[..., None].astype(jnp.float32)
    return jnp.concatenate([real_part * factor, imag_part * factor], axis=-1).astype(jnp.bfloat16)

def rotate(whitened, cosine, sine):
    half = L // 2
    real_part = whitened[..., :half].astype(jnp.float32)
    imag_part = whitened[..., half:].astype(jnp.float32)
    first = real_part * cosine + imag_part * sine
    second = imag_part * cosine - real_part * sine
    return jnp.concatenate([first, second], axis=-1).astype(jnp.bfloat16)

def reference(traces, valid):
    dft_table, cosines, sines = make_tables()
    whitened = whiten(traces, valid, dft_table)
    count = whitened.shape[1]
    left_flat = jnp.transpose(whitened, (1, 0, 2)).reshape(count, -1)
    scale = 1.0 / math.sqrt(traces.shape[0] * (L // 2))

    def one_lag(index):
        rotated = rotate(whitened, cosines[index][None, None, :], sines[index][None, None, :])
        right_flat = jnp.transpose(rotated, (1, 0, 2)).reshape(count, -1)
        sums = jnp.dot(right_flat, left_flat.T, preferred_element_type=jnp.float32)
        return (sums * scale).reshape(N_ROW, count // N_ROW, count)
    return lax.map(one_lag, jnp.arange(2 * MAXLAG + 1, dtype=jnp.int32))
```

```python
import functools
import math

import jax
import jax.numpy as jnp
import numpy as np
from jax import lax
from jax.experimental import pallas as pl
from jax.experimental.pallas import tpu as pltpu
from jax.sharding import PartitionSpec as P

MAXLAG = 16
LAGSET = 3
VMEM = pl.BlockSpec(memory_space=pltpu.VMEM)
SMEM = pl.BlockSpec(memory_space=pltpu.SMEM)


def grant(mib):
    return pltpu.CompilerParams(vmem_limit_bytes=mib * 2**20)


def make_tables(length, max_shift):
    bins = jnp.arange(length // 2, dtype=jnp.int32)
    samples = jnp.arange(length, dtype=jnp.int32)
    product = samples[:, None] * bins[None, :] % length
    angle = 2.0 * math.pi / length * product.astype(jnp.float32)
    dft_table = jnp.concatenate([jnp.cos(angle), -jnp.sin(angle)], axis=1).astype(jnp.bfloat16)
    shifts = jnp.arange(2 * max_shift + 1, dtype=jnp.int32) - max_shift
    lag_prod = shifts[:, None] * bins[None, :] % length
    lag_angle = 2.0 * math.pi / length * lag_prod.astype(jnp.float32)
    return (dft_table, jnp.cos(lag_angle), jnp.sin(lag_angle))


def whiten(traces, valid, dft_table):
    length = traces.shape[2]
    half = length // 2
    flat = traces.reshape(-1, length)
    spectrum = jnp.dot(flat, dft_table, preferred_element_type=jnp.float32)
    spectrum = spectrum.reshape(traces.shape[0], traces.shape[1], length)
    real_part = spectrum[..., :half]
    imag_part = spectrum[..., half:]
    power = real_part * real_part + imag_part * imag_part
    level = jnp.mean(power, axis=-1, keepdims=True)
    factor = lax.rsqrt(power + 0.1 * level + 1e-05) * valid[..., None].astype(jnp.float32)
    return jnp.concatenate([real_part * factor, imag_part * factor], axis=-1).astype(jnp.bfloat16)


def lag_sums(first_set, second_set, cosines, sines, group_size):
    half = first_set.shape[2] // 2
    lag_count = cosines.shape[0]
    real_part = second_set[..., :half].astype(jnp.float32)
    imag_part = second_set[..., half:].astype(jnp.float32)

    def one_group(group):
        cosine = lax.dynamic_slice_in_dim(cosines, group * group_size, group_size, 0)[
            :, None, None, :
        ]
        sine = lax.dynamic_slice_in_dim(sines, group * group_size, group_size, 0)[:, None, None, :]
        first = real_part[None] * cosine + imag_part[None] * sine
        second = imag_part[None] * cosine - real_part[None] * sine
        rotated = jnp.concatenate([first, second], axis=-1).astype(jnp.bfloat16)
        return jnp.einsum("gsbk,sak->gba", rotated, first_set, preferred_element_type=jnp.float32)

    result = lax.map(one_group, jnp.arange(lag_count // group_size, dtype=jnp.int32))
    return result.reshape(lag_count, second_set.shape[1], first_set.shape[1])


def general_device(traces, valid):
    length = traces.shape[2]
    dft_table, cosines, sines = make_tables(length, MAXLAG)
    whitened = whiten(traces, valid, dft_table)
    first_set = lax.all_gather(whitened, "col", axis=1, tiled=True)
    second_set = lax.all_gather(whitened, "row", axis=1, tiled=True)
    groups_row = lax.axis_size("row")
    seg_count = lax.axis_size("seg")
    segments_all = whitened.shape[0] * seg_count
    scale = 1.0 / math.sqrt(segments_all * (length // 2))
    own_count = whitened.shape[1]
    partial_value = lag_sums(first_set, second_set, cosines, sines, LAGSET)
    partial_value = partial_value.reshape(
        partial_value.shape[0], groups_row, own_count, partial_value.shape[2]
    )
    summed = lax.psum_scatter(partial_value, "seg", scatter_dimension=2, tiled=True)
    return summed * scale


def bin_order(length):
    return np.concatenate([np.arange(r, length // 2, 4) for r in range(4)])


def quarter_table(length):
    product = np.arange(length // 4)[:, None] * bin_order(length)[None, :] % length
    angle = 2.0 * np.pi / length * product
    return np.concatenate([np.cos(angle), -np.sin(angle)], axis=1).astype(jnp.bfloat16)


def lag_tables(length, max_shift, copies, rows):
    shifts = np.arange(2 * max_shift + 1) - max_shift
    product = shifts[:, None] * bin_order(length)[None, :] % length
    angle = 2.0 * np.pi / length * product
    out = []
    for table in (np.cos(angle), np.sin(angle)):
        full = np.zeros((rows, length // 2), np.float32)
        full[: copies * len(shifts)] = np.repeat(table, copies, axis=0)
        out.append(full)
    return out


def whiten_kernel(x_ref, v_ref, t_ref, w_ref):
    segs, own, length = x_ref.shape
    quarter, half = length // 4, length // 2
    rows, group = segs * own, half // 4
    stacked = jnp.concatenate(
        [x_ref[:, :, q * quarter : (q + 1) * quarter].reshape(rows, quarter) for q in range(4)],
        axis=0,
    )
    z = jnp.dot(stacked, t_ref[...], preferred_element_type=jnp.float32)

    def piece(q, r, imag):
        start = r * group + (half if imag else 0)
        return z[q * rows : (q + 1) * rows, start : start + group]

    real, imag = [], []
    for r in range(4):
        re, im = piece(0, r, False), piece(0, r, True)
        for q in range(1, 4):
            a, b = piece(q, r, False), piece(q, r, True)
            turn = (q * r) % 4
            if turn == 0:
                re, im = re + a, im + b
            elif turn == 1:
                re, im = re + b, im - a
            elif turn == 2:
                re, im = re - a, im - b
            else:
                re, im = re - b, im + a
        real.append(re)
        imag.append(im)
    power = [re * re + im * im for re, im in zip(real, imag)]
    level = jnp.sum(power[0] + power[1] + power[2] + power[3], axis=-1, keepdims=True) / half
    flags = v_ref[...].astype(jnp.float32)
    eye = lax.broadcasted_iota(jnp.int32, (own, own), 0) == lax.broadcasted_iota(
        jnp.int32, (own, own), 1
    )
    column = jnp.concatenate(
        [
            jnp.sum(
                jnp.where(eye, jnp.broadcast_to(flags[s : s + 1], (own, own)), 0.0),
                axis=-1,
                keepdims=True,
            )
            for s in range(segs)
        ],
        axis=0,
    )
    for r in range(4):
        factor = lax.rsqrt(power[r] + 0.1 * level + 1e-05) * column
        for base, part in ((0, real[r]), (half, imag[r])):
            value = (part * factor).astype(jnp.bfloat16).reshape(segs, own, group)
            w_ref[:, :, base + r * group : base + (r + 1) * group] = value


def rotate_kernel(seg_ref, w_ref, c_ref, s_ref, r_ref):
    segs, own, length = w_ref.shape
    half, part = length // 2, own // 2
    rows = c_ref.shape[0]
    first_half = seg_ref[0] == 0
    for seg in range(segs):
        w = w_ref[seg].astype(jnp.float32)
        low, high = w[:part], w[part:]
        keep = jnp.where(first_half, low, high)
        send = jnp.where(first_half, high, low)
        keep2 = jnp.concatenate([keep, keep], axis=0)
        send2 = jnp.concatenate([send, send], axis=0)
        for start in range(0, 2 * rows, 2 * own):
            pieces = []
            for row in (start, start + own):
                w2 = keep2 if row < rows else send2
                at = row % rows
                pieces.append((w2[:, :half], w2[:, half:], at))
            top, bottom = [], []
            for re, im, at in pieces:
                c, s = c_ref[at : at + own], s_ref[at : at + own]
                top.append(re * c + im * s)
                bottom.append(im * c - re * s)
            stop = start + 2 * own
            r_ref[seg, start:stop, :half] = jnp.concatenate(top, axis=0).astype(jnp.bfloat16)
            r_ref[seg, start:stop, half:] = jnp.concatenate(bottom, axis=0).astype(jnp.bfloat16)


def correlate_kernel(*refs):
    r_ref, keep_ref, send_ref = refs[0], refs[-2], refs[-1]
    blocks = refs[1:-2]
    rows = keep_ref.shape[0]
    total = None
    for seg in range(r_ref.shape[0]):
        first = jnp.concatenate([b[seg] for b in blocks], axis=0)
        term = lax.dot_general(
            r_ref[seg], first, (((1,), (1,)), ((), ())), preferred_element_type=jnp.float32
        )
        total = term if total is None else total + term
    keep_ref[...] = total[:rows]
    send_ref[...] = total[rows:]


def finish_kernel(scale, own, me_ref, keep_ref, got_ref, out_ref):
    lags, part, lanes = out_ref.shape
    value = (keep_ref[: lags * part] + got_ref[: lags * part]) * scale
    lane = lax.broadcasted_iota(jnp.int32, value.shape, 1)
    width = own
    bit = 1
    while width < lanes:
        up = pltpu.roll(value, width, 1)
        down = pltpu.roll(value, lanes - width, 1)
        swapped = jnp.where((lane & width) != 0, up, down)
        value = jnp.where((me_ref[0] & bit) != 0, swapped, value)
        width, bit = 2 * width, 2 * bit
    for lag in range(lags):
        out_ref[lag] = value[lag * part : (lag + 1) * part]


def fast_device(traces, valid):
    segs, own, length = traces.shape
    col = lax.axis_size("col")
    lags, part, lanes = 2 * MAXLAG + 1, own // 2, own * col
    half = length // 2
    rows = -(-lags * part // own) * own
    me = lax.axis_index("col").astype(jnp.int32).reshape(1)
    seg_index = lax.axis_index("seg").astype(jnp.int32).reshape(1)
    scale = 1.0 / math.sqrt(segs * lax.axis_size("seg") * half)

    with jax.named_scope("whiten"):
        whitened = pl.pallas_call(
            whiten_kernel,
            out_shape=jax.ShapeDtypeStruct(traces.shape, jnp.bfloat16),
            in_specs=[VMEM] * 3,
            out_specs=VMEM,
            compiler_params=grant(4),
        )(traces, valid, jnp.asarray(quarter_table(length)))

    blocks = {0: whitened}
    bit = col // 2
    while bit:
        for held in list(blocks):
            with jax.named_scope(f"move{held | bit}"):
                blocks[held | bit] = lax.ppermute(
                    blocks[held], "col", [(i, i ^ bit) for i in range(col)]
                )
        bit //= 2

    cosines, sines = lag_tables(length, MAXLAG, part, rows)
    with jax.named_scope("rotate"):
        rotated = pl.pallas_call(
            rotate_kernel,
            out_shape=jax.ShapeDtypeStruct((segs, 2 * rows, length), jnp.bfloat16),
            in_specs=[SMEM, VMEM, VMEM, VMEM],
            out_specs=VMEM,
            compiler_params=grant(8),
            cost_estimate=pl.CostEstimate(
                flops=12 * segs * rows * length, bytes_accessed=4 * segs * rows * length, transcendentals=0
            ),
        )(seg_index, whitened, jnp.asarray(cosines), jnp.asarray(sines))

    with jax.named_scope("correlate"):
        keep, send = pl.pallas_call(
            correlate_kernel,
            out_shape=[jax.ShapeDtypeStruct((rows, lanes), jnp.float32)] * 2,
            in_specs=[VMEM] * (1 + col),
            out_specs=[VMEM] * 2,
            compiler_params=grant(12),
        )(rotated, *[blocks[m] for m in range(col)])
    with jax.named_scope("trade"):
        got = lax.ppermute(send, "seg", [(0, 1), (1, 0)])
    with jax.named_scope("finish"):
        out = pl.pallas_call(
            functools.partial(finish_kernel, scale, own),
            out_shape=jax.ShapeDtypeStruct((lags, part, lanes), jnp.float32),
            in_specs=[SMEM, VMEM, VMEM],
            out_specs=VMEM,
            compiler_params=grant(2),
        )(me, keep, got)
    return out[:, None]


def on_device(traces, valid):
    col = lax.axis_size("col")
    fast = (
        lax.axis_size("row") == 1
        and lax.axis_size("seg") == 2
        and col & (col - 1) == 0
        and traces.shape[1] == 8
        and traces.shape[1] * col == 128
        and traces.shape[2] % 1024 == 0
    )
    return (fast_device if fast else general_device)(traces, valid)


def solution(mesh):
    placed = (P("seg", ("row", "col"), None), P("seg", ("row", "col")))
    return jax.shard_map(
        on_device,
        mesh=mesh,
        in_specs=placed,
        out_specs=P(None, None, ("col", "seg"), "row"),
        check_vma=False,
    )
```

```python
import functools
import math

import jax
import jax.numpy as jnp
import numpy as np
from jax import lax
from jax.experimental import pallas as pl
from jax.experimental.pallas import tpu as pltpu
from jax.sharding import PartitionSpec as P

MAXLAG = 16
LAGSET = 3
VMEM = pl.BlockSpec(memory_space=pltpu.VMEM)
SMEM = pl.BlockSpec(memory_space=pltpu.SMEM)
HBM = pl.BlockSpec(memory_space=pltpu.HBM)


def grant(mib):
    return pltpu.CompilerParams(vmem_limit_bytes=mib * 2**20)


def make_tables(length, max_shift):
    bins = jnp.arange(length // 2, dtype=jnp.int32)
    samples = jnp.arange(length, dtype=jnp.int32)
    product = samples[:, None] * bins[None, :] % length
    angle = 2.0 * math.pi / length * product.astype(jnp.float32)
    dft_table = jnp.concatenate([jnp.cos(angle), -jnp.sin(angle)], axis=1).astype(jnp.bfloat16)
    shifts = jnp.arange(2 * max_shift + 1, dtype=jnp.int32) - max_shift
    lag_prod = shifts[:, None] * bins[None, :] % length
    lag_angle = 2.0 * math.pi / length * lag_prod.astype(jnp.float32)
    return (dft_table, jnp.cos(lag_angle), jnp.sin(lag_angle))


def whiten(traces, valid, dft_table):
    length = traces.shape[2]
    half = length // 2
    flat = traces.reshape(-1, length)
    spectrum = jnp.dot(flat, dft_table, preferred_element_type=jnp.float32)
    spectrum = spectrum.reshape(traces.shape[0], traces.shape[1], length)
    real_part = spectrum[..., :half]
    imag_part = spectrum[..., half:]
    power = real_part * real_part + imag_part * imag_part
    level = jnp.mean(power, axis=-1, keepdims=True)
    factor = lax.rsqrt(power + 0.1 * level + 1e-05) * valid[..., None].astype(jnp.float32)
    return jnp.concatenate([real_part * factor, imag_part * factor], axis=-1).astype(jnp.bfloat16)


def lag_sums(first_set, second_set, cosines, sines, group_size):
    half = first_set.shape[2] // 2
    lag_count = cosines.shape[0]
    real_part = second_set[..., :half].astype(jnp.float32)
    imag_part = second_set[..., half:].astype(jnp.float32)

    def one_group(group):
        cosine = lax.dynamic_slice_in_dim(cosines, group * group_size, group_size, 0)[
            :, None, None, :
        ]
        sine = lax.dynamic_slice_in_dim(sines, group * group_size, group_size, 0)[:, None, None, :]
        first = real_part[None] * cosine + imag_part[None] * sine
        second = imag_part[None] * cosine - real_part[None] * sine
        rotated = jnp.concatenate([first, second], axis=-1).astype(jnp.bfloat16)
        return jnp.einsum("gsbk,sak->gba", rotated, first_set, preferred_element_type=jnp.float32)

    result = lax.map(one_group, jnp.arange(lag_count // group_size, dtype=jnp.int32))
    return result.reshape(lag_count, second_set.shape[1], first_set.shape[1])


def general_device(traces, valid):
    length = traces.shape[2]
    dft_table, cosines, sines = make_tables(length, MAXLAG)
    whitened = whiten(traces, valid, dft_table)
    first_set = lax.all_gather(whitened, "col", axis=1, tiled=True)
    second_set = lax.all_gather(whitened, "row", axis=1, tiled=True)
    groups_row = lax.axis_size("row")
    seg_count = lax.axis_size("seg")
    segments_all = whitened.shape[0] * seg_count
    scale = 1.0 / math.sqrt(segments_all * (length // 2))
    own_count = whitened.shape[1]
    partial_value = lag_sums(first_set, second_set, cosines, sines, LAGSET)
    partial_value = partial_value.reshape(
        partial_value.shape[0], groups_row, own_count, partial_value.shape[2]
    )
    summed = lax.psum_scatter(partial_value, "seg", scatter_dimension=2, tiled=True)
    return summed * scale


def bin_order(length):
    return np.concatenate([np.arange(r, length // 2, 4) for r in range(4)])


def quarter_table(length):
    product = np.arange(length // 4)[:, None] * bin_order(length)[None, :] % length
    angle = 2.0 * np.pi / length * product
    return np.concatenate([np.cos(angle), -np.sin(angle)], axis=1).astype(jnp.bfloat16)


def lag_tables(length, max_shift, copies, rows):
    shifts = np.arange(2 * max_shift + 1) - max_shift
    product = shifts[:, None] * bin_order(length)[None, :] % length
    angle = 2.0 * np.pi / length * product
    out = []
    for table in (np.cos(angle), np.sin(angle)):
        full = np.zeros((rows, length // 2), np.float32)
        full[: copies * len(shifts)] = np.repeat(table, copies, axis=0)
        out.append(full)
    return out


def whiten_kernel(
    x_in, v_in, t_in, c_in, s_in, w_ref, c_out, s_out, x_ref, v_ref, t_ref, sems
):
    pairs = ((x_in, x_ref), (t_in, t_ref), (v_in, v_ref), (c_in, c_out), (s_in, s_out))
    copies = [pltpu.make_async_copy(a, b, sems.at[i]) for i, (a, b) in enumerate(pairs)]
    for copy in copies:
        copy.start()
    segs, own, length = x_ref.shape
    for copy in copies[:3]:
        copy.wait()
    quarter, half = length // 4, length // 2
    rows, group = segs * own, half // 4
    stacked = jnp.concatenate(
        [x_ref[:, :, q * quarter : (q + 1) * quarter].reshape(rows, quarter) for q in range(4)],
        axis=0,
    )
    z = jnp.dot(stacked, t_ref[...], preferred_element_type=jnp.float32)

    def piece(q, r, imag):
        start = r * group + (half if imag else 0)
        return z[q * rows : (q + 1) * rows, start : start + group]

    real, imag = [], []
    for r in range(4):
        re, im = piece(0, r, False), piece(0, r, True)
        for q in range(1, 4):
            a, b = piece(q, r, False), piece(q, r, True)
            turn = (q * r) % 4
            if turn == 0:
                re, im = re + a, im + b
            elif turn == 1:
                re, im = re + b, im - a
            elif turn == 2:
                re, im = re - a, im - b
            else:
                re, im = re - b, im + a
        real.append(re)
        imag.append(im)
    power = [re * re + im * im for re, im in zip(real, imag)]
    level = jnp.sum(power[0] + power[1] + power[2] + power[3], axis=-1, keepdims=True) / half
    flags = v_ref[...].astype(jnp.float32)
    eye = lax.broadcasted_iota(jnp.int32, (own, own), 0) == lax.broadcasted_iota(
        jnp.int32, (own, own), 1
    )
    column = jnp.concatenate(
        [
            jnp.sum(
                jnp.where(eye, jnp.broadcast_to(flags[s : s + 1], (own, own)), 0.0),
                axis=-1,
                keepdims=True,
            )
            for s in range(segs)
        ],
        axis=0,
    )
    for r in range(4):
        factor = lax.rsqrt(power[r] + 0.1 * level + 1e-05) * column
        for base, part in ((0, real[r]), (half, imag[r])):
            value = (part * factor).astype(jnp.bfloat16).reshape(segs, own, group)
            w_ref[:, :, base + r * group : base + (r + 1) * group] = value
    for copy in copies[3:]:
        copy.wait()


def rotate_kernel(seg_ref, w_ref, c_ref, s_ref, r_ref):
    segs, own, length = w_ref.shape
    half, part = length // 2, own // 2
    rows = c_ref.shape[0]
    first_half = seg_ref[0] == 0
    for seg in range(segs):
        w = w_ref[seg].astype(jnp.float32)
        low, high = w[:part], w[part:]
        keep = jnp.where(first_half, low, high)
        send = jnp.where(first_half, high, low)
        keep2 = jnp.concatenate([keep, keep], axis=0)
        send2 = jnp.concatenate([send, send], axis=0)
        for start in range(0, 2 * rows, 2 * own):
            pieces = []
            for row in (start, start + own):
                w2 = keep2 if row < rows else send2
                at = row % rows
                pieces.append((w2[:, :half], w2[:, half:], at))
            top, bottom = [], []
            for re, im, at in pieces:
                c, s = c_ref[at : at + own], s_ref[at : at + own]
                top.append(re * c + im * s)
                bottom.append(im * c - re * s)
            stop = start + 2 * own
            r_ref[seg, start:stop, :half] = jnp.concatenate(top, axis=0).astype(jnp.bfloat16)
            r_ref[seg, start:stop, half:] = jnp.concatenate(bottom, axis=0).astype(jnp.bfloat16)


def correlate_kernel(*refs):
    r_ref, keep_ref, send_ref = refs[0], refs[-2], refs[-1]
    blocks = refs[1:-2]
    rows = keep_ref.shape[0]
    total = None
    for seg in range(r_ref.shape[0]):
        first = jnp.concatenate([b[seg] for b in blocks], axis=0)
        term = lax.dot_general(
            r_ref[seg], first, (((1,), (1,)), ((), ())), preferred_element_type=jnp.float32
        )
        total = term if total is None else total + term
    keep_ref[...] = total[:rows]
    send_ref[...] = total[rows:]


def finish_kernel(scale, own, me_ref, keep_ref, got_ref, out_ref):
    lags, part, lanes = out_ref.shape
    value = (keep_ref[: lags * part] + got_ref[: lags * part]) * scale
    lane = lax.broadcasted_iota(jnp.int32, value.shape, 1)
    width = own
    bit = 1
    while width < lanes:
        up = pltpu.roll(value, width, 1)
        down = pltpu.roll(value, lanes - width, 1)
        swapped = jnp.where((lane & width) != 0, up, down)
        value = jnp.where((me_ref[0] & bit) != 0, swapped, value)
        width, bit = 2 * width, 2 * bit
    for lag in range(lags):
        out_ref[lag] = value[lag * part : (lag + 1) * part]


def gather_plan(col):
    bits = [1 << i for i in reversed(range(col.bit_length() - 1))]
    far, close, last = bits[:-3], bits[-3:-1], bits[-1:]
    held, steps = [0], []
    for bit in far:
        steps += [(m | bit, m, bit) for m in held]
        held += [m | bit for m in held]
    near = [sum(close)] * (len(close) > 1) + close
    for m in list(held):
        steps += [(m | d, m, d) for d in near]
        held += [m | d for d in near]
    for bit in last:
        steps += [(m | bit, m, bit) for m in held]
    return steps


def fast_device(traces, valid):
    return fast_body(traces, valid)


def fast_body(traces, valid):
    segs, own, length = traces.shape
    col = lax.axis_size("col")
    lags, part, lanes = 2 * MAXLAG + 1, own // 2, own * col
    half = length // 2
    rows = -(-lags * part // own) * own
    me = lax.axis_index("col").astype(jnp.int32).reshape(1)
    seg_index = lax.axis_index("seg").astype(jnp.int32).reshape(1)
    scale = 1.0 / math.sqrt(segs * lax.axis_size("seg") * half)

    table = quarter_table(length)
    lag_cos, lag_sin = lag_tables(length, MAXLAG, part, rows)
    whitened, cosines, sines = pl.pallas_call(
        whiten_kernel,
        out_shape=[
            jax.ShapeDtypeStruct(traces.shape, jnp.bfloat16),
            jax.ShapeDtypeStruct(lag_cos.shape, jnp.float32),
            jax.ShapeDtypeStruct(lag_sin.shape, jnp.float32),
        ],
        in_specs=[HBM] * 5,
        out_specs=[VMEM] * 3,
        scratch_shapes=[
            pltpu.VMEM(traces.shape, traces.dtype),
            pltpu.VMEM(valid.shape, valid.dtype),
            pltpu.VMEM(table.shape, table.dtype),
            pltpu.SemaphoreType.DMA((5,)),
        ],
        compiler_params=grant(4),
    )(
        *[
            pltpu.with_memory_space_constraint(jnp.asarray(t), pltpu.HBM)
            for t in (traces, valid, table, lag_cos, lag_sin)
        ]
    )

    blocks = {0: whitened}
    for block, held, distance in gather_plan(col):
        blocks[block] = lax.ppermute(blocks[held], "col", [(i, i ^ distance) for i in range(col)])

    rotated = pl.pallas_call(
        rotate_kernel,
        out_shape=jax.ShapeDtypeStruct((segs, 2 * rows, length), jnp.bfloat16),
        in_specs=[SMEM, VMEM, VMEM, VMEM],
        out_specs=VMEM,
        compiler_params=grant(8),
        cost_estimate=pl.CostEstimate(
            flops=12 * segs * rows * length,
            bytes_accessed=4 * segs * rows * length,
            transcendentals=0,
        ),
    )(seg_index, whitened, cosines, sines)

    keep, send = pl.pallas_call(
        correlate_kernel,
        out_shape=[jax.ShapeDtypeStruct((rows, lanes), jnp.float32)] * 2,
        in_specs=[VMEM] * (1 + col),
        out_specs=[VMEM] * 2,
        compiler_params=grant(12),
    )(rotated, *[blocks[m] for m in range(col)])
    got = lax.ppermute(send, "seg", [(0, 1), (1, 0)])
    out = pl.pallas_call(
        functools.partial(finish_kernel, scale, own),
        out_shape=jax.ShapeDtypeStruct((lags, part, lanes), jnp.float32),
        in_specs=[SMEM, VMEM, VMEM],
        out_specs=VMEM,
        compiler_params=grant(2),
    )(me, keep, got)
    return out[:, None]


def on_device(traces, valid):
    fast = (
        fast_mesh(lax.axis_size("row"), lax.axis_size("col"), lax.axis_size("seg"))
        and traces.shape[1] == 8
        and traces.shape[1] * lax.axis_size("col") == 128
        and traces.shape[2] % 1024 == 0
    )
    return (fast_device if fast else general_device)(traces, valid)


def fast_mesh(row, col, seg):
    return row == 1 and seg == 2 and col >= 8 and col & (col - 1) == 0


def solution(mesh):
    placed = (P("seg", ("row", "col"), None), P("seg", ("row", "col")))
    return jax.shard_map(
        on_device,
        mesh=mesh,
        in_specs=placed,
        out_specs=P(None, None, ("col", "seg"), "row"),
        check_vma=False,
    )
```

```python
import functools
import math

import jax
import jax.numpy as jnp
import numpy as np
from jax import lax
from jax.experimental import pallas as pl
from jax.experimental.pallas import tpu as pltpu
from jax.sharding import PartitionSpec as P

MAXLAG = 16
LAGSET = 3
VMEM = pl.BlockSpec(memory_space=pltpu.VMEM)
SMEM = pl.BlockSpec(memory_space=pltpu.SMEM)
HBM = pl.BlockSpec(memory_space=pltpu.HBM)


def grant(mib):
    return pltpu.CompilerParams(vmem_limit_bytes=mib * 2**20)


def make_tables(length, max_shift):
    bins = jnp.arange(length // 2, dtype=jnp.int32)
    samples = jnp.arange(length, dtype=jnp.int32)
    product = samples[:, None] * bins[None, :] % length
    angle = 2.0 * math.pi / length * product.astype(jnp.float32)
    dft_table = jnp.concatenate([jnp.cos(angle), -jnp.sin(angle)], axis=1).astype(jnp.bfloat16)
    shifts = jnp.arange(2 * max_shift + 1, dtype=jnp.int32) - max_shift
    lag_prod = shifts[:, None] * bins[None, :] % length
    lag_angle = 2.0 * math.pi / length * lag_prod.astype(jnp.float32)
    return (dft_table, jnp.cos(lag_angle), jnp.sin(lag_angle))


def whiten(traces, valid, dft_table):
    length = traces.shape[2]
    half = length // 2
    flat = traces.reshape(-1, length)
    spectrum = jnp.dot(flat, dft_table, preferred_element_type=jnp.float32)
    spectrum = spectrum.reshape(traces.shape[0], traces.shape[1], length)
    real_part = spectrum[..., :half]
    imag_part = spectrum[..., half:]
    power = real_part * real_part + imag_part * imag_part
    level = jnp.mean(power, axis=-1, keepdims=True)
    factor = lax.rsqrt(power + 0.1 * level + 1e-05) * valid[..., None].astype(jnp.float32)
    return jnp.concatenate([real_part * factor, imag_part * factor], axis=-1).astype(jnp.bfloat16)


def lag_sums(first_set, second_set, cosines, sines, group_size):
    half = first_set.shape[2] // 2
    lag_count = cosines.shape[0]
    real_part = second_set[..., :half].astype(jnp.float32)
    imag_part = second_set[..., half:].astype(jnp.float32)

    def one_group(group):
        cosine = lax.dynamic_slice_in_dim(cosines, group * group_size, group_size, 0)[
            :, None, None, :
        ]
        sine = lax.dynamic_slice_in_dim(sines, group * group_size, group_size, 0)[:, None, None, :]
        first = real_part[None] * cosine + imag_part[None] * sine
        second = imag_part[None] * cosine - real_part[None] * sine
        rotated = jnp.concatenate([first, second], axis=-1).astype(jnp.bfloat16)
        return jnp.einsum("gsbk,sak->gba", rotated, first_set, preferred_element_type=jnp.float32)

    result = lax.map(one_group, jnp.arange(lag_count // group_size, dtype=jnp.int32))
    return result.reshape(lag_count, second_set.shape[1], first_set.shape[1])


def general_device(traces, valid):
    length = traces.shape[2]
    dft_table, cosines, sines = make_tables(length, MAXLAG)
    whitened = whiten(traces, valid, dft_table)
    first_set = lax.all_gather(whitened, "col", axis=1, tiled=True)
    second_set = lax.all_gather(whitened, "row", axis=1, tiled=True)
    groups_row = lax.axis_size("row")
    seg_count = lax.axis_size("seg")
    segments_all = whitened.shape[0] * seg_count
    scale = 1.0 / math.sqrt(segments_all * (length // 2))
    own_count = whitened.shape[1]
    partial_value = lag_sums(first_set, second_set, cosines, sines, LAGSET)
    partial_value = partial_value.reshape(
        partial_value.shape[0], groups_row, own_count, partial_value.shape[2]
    )
    summed = lax.psum_scatter(partial_value, "seg", scatter_dimension=2, tiled=True)
    return summed * scale


def bin_order(length):
    return np.concatenate([np.arange(r, length // 2, 4) for r in range(4)])


def quarter_table(length):
    product = np.arange(length // 4)[:, None] * bin_order(length)[None, :] % length
    angle = 2.0 * np.pi / length * product
    return np.concatenate([np.cos(angle), -np.sin(angle)], axis=1).astype(jnp.bfloat16)


def lag_tables(length, max_shift, copies, rows):
    shifts = np.arange(2 * max_shift + 1) - max_shift
    product = shifts[:, None] * bin_order(length)[None, :] % length
    angle = 2.0 * np.pi / length * product
    out = []
    for table in (np.cos(angle), np.sin(angle)):
        full = np.zeros((rows, length // 2), np.float32)
        full[: copies * len(shifts)] = np.repeat(table, copies, axis=0)
        out.append(full)
    return out


def whiten_kernel(
    x_in, v_in, t_in, c_in, s_in, w_ref, c_out, s_out, x_ref, v_ref, t_ref, sems
):
    pairs = ((x_in, x_ref), (t_in, t_ref), (v_in, v_ref), (c_in, c_out), (s_in, s_out))
    copies = [pltpu.make_async_copy(a, b, sems.at[i]) for i, (a, b) in enumerate(pairs)]
    for copy in copies:
        copy.start()
    segs, own, length = x_ref.shape
    for copy in copies[:3]:
        copy.wait()
    quarter, half = length // 4, length // 2
    rows, group = segs * own, half // 4
    stacked = jnp.concatenate(
        [x_ref[:, :, q * quarter : (q + 1) * quarter].reshape(rows, quarter) for q in range(4)],
        axis=0,
    )
    z = jnp.dot(stacked, t_ref[...], preferred_element_type=jnp.float32)

    def piece(q, r, imag):
        start = r * group + (half if imag else 0)
        return z[q * rows : (q + 1) * rows, start : start + group]

    real, imag = [], []
    for r in range(4):
        re, im = piece(0, r, False), piece(0, r, True)
        for q in range(1, 4):
            a, b = piece(q, r, False), piece(q, r, True)
            turn = (q * r) % 4
            if turn == 0:
                re, im = re + a, im + b
            elif turn == 1:
                re, im = re + b, im - a
            elif turn == 2:
                re, im = re - a, im - b
            else:
                re, im = re - b, im + a
        real.append(re)
        imag.append(im)
    power = [re * re + im * im for re, im in zip(real, imag)]
    level = jnp.sum(power[0] + power[1] + power[2] + power[3], axis=-1, keepdims=True) / half
    flags = v_ref[...].astype(jnp.float32)
    eye = lax.broadcasted_iota(jnp.int32, (own, own), 0) == lax.broadcasted_iota(
        jnp.int32, (own, own), 1
    )
    column = jnp.concatenate(
        [
            jnp.sum(
                jnp.where(eye, jnp.broadcast_to(flags[s : s + 1], (own, own)), 0.0),
                axis=-1,
                keepdims=True,
            )
            for s in range(segs)
        ],
        axis=0,
    )
    for r in range(4):
        factor = lax.rsqrt(power[r] + 0.1 * level + 1e-05) * column
        for base, part in ((0, real[r]), (half, imag[r])):
            value = (part * factor).astype(jnp.bfloat16).reshape(segs, own, group)
            w_ref[:, :, base + r * group : base + (r + 1) * group] = value
    for copy in copies[3:]:
        copy.wait()


def rotate_kernel(seg_ref, w_ref, c_ref, s_ref, r_ref):
    segs, own, length = w_ref.shape
    half, part = length // 2, own // 2
    rows = c_ref.shape[0]
    first_half = seg_ref[0] == 0
    for seg in range(segs):
        w = w_ref[seg].astype(jnp.float32)
        low, high = w[:part], w[part:]
        keep = jnp.where(first_half, low, high)
        send = jnp.where(first_half, high, low)
        keep2 = jnp.concatenate([keep, keep], axis=0)
        send2 = jnp.concatenate([send, send], axis=0)
        for start in range(0, 2 * rows, 2 * own):
            pieces = []
            for row in (start, start + own):
                w2 = keep2 if row < rows else send2
                at = row % rows
                pieces.append((w2[:, :half], w2[:, half:], at))
            top, bottom = [], []
            for re, im, at in pieces:
                c, s = c_ref[at : at + own], s_ref[at : at + own]
                top.append(re * c + im * s)
                bottom.append(im * c - re * s)
            stop = start + 2 * own
            r_ref[seg, start:stop, :half] = jnp.concatenate(top, axis=0).astype(jnp.bfloat16)
            r_ref[seg, start:stop, half:] = jnp.concatenate(bottom, axis=0).astype(jnp.bfloat16)


def correlate_kernel(*refs):
    r_ref, keep_ref, send_ref = refs[0], refs[-2], refs[-1]
    blocks = refs[1:-2]
    rows = keep_ref.shape[0]
    total = None
    for seg in range(r_ref.shape[0]):
        first = []
        for at in range(0, len(blocks), 6):
            block, mate, pair_mate, pair, cross, cross_mate = blocks[at : at + 6]
            first += [block[seg], mate[seg], pair_mate[1, seg], pair_mate[0, seg]]
            first += [pair[0, seg], pair[1, seg], cross[seg], cross_mate[seg]]
        first = jnp.concatenate(first, axis=0)
        term = lax.dot_general(
            r_ref[seg], first, (((1,), (1,)), ((), ())), preferred_element_type=jnp.float32
        )
        total = term if total is None else total + term
    keep_ref[...] = total[:rows]
    send_ref[...] = total[rows:]


def pair_kernel(a_ref, b_ref, out_ref):
    out_ref[0] = a_ref[...]
    out_ref[1] = b_ref[...]


def finish_kernel(scale, own, me_ref, keep_ref, got_ref, out_ref):
    lags, part, lanes = out_ref.shape
    value = (keep_ref[: lags * part] + got_ref[: lags * part]) * scale
    lane = lax.broadcasted_iota(jnp.int32, value.shape, 1)
    low, high = (lane & (2 * own)) != 0, (lane & (4 * own)) != 0
    after, before = pltpu.roll(value, lanes - 2 * own, 1), pltpu.roll(value, 2 * own, 1)
    crossed = jnp.where(low & ~high, after, jnp.where(high & ~low, before, value))
    value = jnp.where((me_ref[0] & 1) != 0, crossed, value)
    width = own
    bit = 1
    while width < lanes:
        up = pltpu.roll(value, width, 1)
        down = pltpu.roll(value, lanes - width, 1)
        swapped = jnp.where((lane & width) != 0, up, down)
        value = jnp.where((me_ref[0] & bit) != 0, swapped, value)
        width, bit = 2 * width, 2 * bit
    for lag in range(lags):
        out_ref[lag] = value[lag * part : (lag + 1) * part]


CORE, SIDE, NEAR = 1, 2, 4


def far_blocks(col):
    held, steps = [0], []
    bit = col // 2
    while bit > NEAR:
        steps += [(m | bit, m, bit) for m in held]
        held += [m | bit for m in held]
        bit //= 2
    return held, steps


def hop(array, col, distance, other=None):
    other = distance if other is None else other
    return lax.ppermute(array, "col", [(i, i ^ (other if i & 1 else distance)) for i in range(col)])


def gather(own_block, col):
    def swap(array):
        return hop(array, col, CORE)

    blocks = {0: own_block}
    held, steps = far_blocks(col)
    for block, source, distance in steps:
        blocks[block] = hop(blocks[source], col, distance)
    out = []
    for m in held:
        block = blocks[m]
        mate = swap(block)
        cross = hop(block, col, NEAR | SIDE)
        pair = pl.pallas_call(
            pair_kernel,
            out_shape=jax.ShapeDtypeStruct((2, *block.shape), block.dtype),
            in_specs=[VMEM] * 2,
            out_specs=VMEM,
            compiler_params=grant(2),
        )(block, mate)
        pair = hop(pair, col, NEAR, SIDE)
        out += [block, mate, swap(pair), pair, cross, swap(cross)]
    return out


def fast_device(traces, valid):
    return fast_body(traces, valid)


def fast_body(traces, valid):
    segs, own, length = traces.shape
    col = lax.axis_size("col")
    lags, part, lanes = 2 * MAXLAG + 1, own // 2, own * col
    half = length // 2
    rows = -(-lags * part // own) * own
    me = lax.axis_index("col").astype(jnp.int32).reshape(1)
    seg_index = lax.axis_index("seg").astype(jnp.int32).reshape(1)
    scale = 1.0 / math.sqrt(segs * lax.axis_size("seg") * half)

    table = quarter_table(length)
    lag_cos, lag_sin = lag_tables(length, MAXLAG, part, rows)
    whitened, cosines, sines = pl.pallas_call(
        whiten_kernel,
        out_shape=[
            jax.ShapeDtypeStruct(traces.shape, jnp.bfloat16),
            jax.ShapeDtypeStruct(lag_cos.shape, jnp.float32),
            jax.ShapeDtypeStruct(lag_sin.shape, jnp.float32),
        ],
        in_specs=[HBM] * 5,
        out_specs=[VMEM] * 3,
        scratch_shapes=[
            pltpu.VMEM(traces.shape, traces.dtype),
            pltpu.VMEM(valid.shape, valid.dtype),
            pltpu.VMEM(table.shape, table.dtype),
            pltpu.SemaphoreType.DMA((5,)),
        ],
        compiler_params=grant(4),
    )(
        *[
            pltpu.with_memory_space_constraint(jnp.asarray(t), pltpu.HBM)
            for t in (traces, valid, table, lag_cos, lag_sin)
        ]
    )

    blocks = gather(whitened, col)

    rotated = pl.pallas_call(
        rotate_kernel,
        out_shape=jax.ShapeDtypeStruct((segs, 2 * rows, length), jnp.bfloat16),
        in_specs=[SMEM, VMEM, VMEM, VMEM],
        out_specs=VMEM,
        compiler_params=grant(8),
        cost_estimate=pl.CostEstimate(
            flops=12 * segs * rows * length,
            bytes_accessed=4 * segs * rows * length,
            transcendentals=0,
        ),
    )(seg_index, whitened, cosines, sines)

    keep, send = pl.pallas_call(
        correlate_kernel,
        out_shape=[jax.ShapeDtypeStruct((rows, lanes), jnp.float32)] * 2,
        in_specs=[VMEM] * (1 + len(blocks)),
        out_specs=[VMEM] * 2,
        compiler_params=grant(12),
    )(rotated, *blocks)
    got = lax.ppermute(send, "seg", [(0, 1), (1, 0)])
    out = pl.pallas_call(
        functools.partial(finish_kernel, scale, own),
        out_shape=jax.ShapeDtypeStruct((lags, part, lanes), jnp.float32),
        in_specs=[SMEM, VMEM, VMEM],
        out_specs=VMEM,
        compiler_params=grant(2),
    )(me, keep, got)
    return out[:, None]


def on_device(traces, valid):
    fast = (
        fast_mesh(lax.axis_size("row"), lax.axis_size("col"), lax.axis_size("seg"))
        and traces.shape[1] == 8
        and traces.shape[1] * lax.axis_size("col") == 128
        and traces.shape[2] % 1024 == 0
    )
    return (fast_device if fast else general_device)(traces, valid)


def fast_mesh(row, col, seg):
    return row == 1 and seg == 2 and col >= 8 and col & (col - 1) == 0


def solution(mesh):
    placed = (P("seg", ("row", "col"), None), P("seg", ("row", "col")))
    return jax.shard_map(
        on_device,
        mesh=mesh,
        in_specs=placed,
        out_specs=P(None, None, ("col", "seg"), "row"),
        check_vma=False,
    )
```

```python
import functools
import math

import jax
import jax.numpy as jnp
import numpy as np
from jax import lax
from jax.experimental import pallas as pl
from jax.experimental.pallas import tpu as pltpu
from jax.sharding import PartitionSpec as P

MAXLAG = 16
LAGSET = 3
VMEM = pl.BlockSpec(memory_space=pltpu.VMEM)
SMEM = pl.BlockSpec(memory_space=pltpu.SMEM)
HBM = pl.BlockSpec(memory_space=pltpu.HBM)


def grant(mib):
    return pltpu.CompilerParams(vmem_limit_bytes=mib * 2**20)


def make_tables(length, max_shift):
    bins = jnp.arange(length // 2, dtype=jnp.int32)
    samples = jnp.arange(length, dtype=jnp.int32)
    product = samples[:, None] * bins[None, :] % length
    angle = 2.0 * math.pi / length * product.astype(jnp.float32)
    dft_table = jnp.concatenate([jnp.cos(angle), -jnp.sin(angle)], axis=1).astype(jnp.bfloat16)
    shifts = jnp.arange(2 * max_shift + 1, dtype=jnp.int32) - max_shift
    lag_prod = shifts[:, None] * bins[None, :] % length
    lag_angle = 2.0 * math.pi / length * lag_prod.astype(jnp.float32)
    return (dft_table, jnp.cos(lag_angle), jnp.sin(lag_angle))


def whiten(traces, valid, dft_table):
    length = traces.shape[2]
    half = length // 2
    flat = traces.reshape(-1, length)
    spectrum = jnp.dot(flat, dft_table, preferred_element_type=jnp.float32)
    spectrum = spectrum.reshape(traces.shape[0], traces.shape[1], length)
    real_part = spectrum[..., :half]
    imag_part = spectrum[..., half:]
    power = real_part * real_part + imag_part * imag_part
    level = jnp.mean(power, axis=-1, keepdims=True)
    factor = lax.rsqrt(power + 0.1 * level + 1e-05) * valid[..., None].astype(jnp.float32)
    return jnp.concatenate([real_part * factor, imag_part * factor], axis=-1).astype(jnp.bfloat16)


def lag_sums(first_set, second_set, cosines, sines, group_size):
    half = first_set.shape[2] // 2
    lag_count = cosines.shape[0]
    real_part = second_set[..., :half].astype(jnp.float32)
    imag_part = second_set[..., half:].astype(jnp.float32)

    def one_group(group):
        cosine = lax.dynamic_slice_in_dim(cosines, group * group_size, group_size, 0)[
            :, None, None, :
        ]
        sine = lax.dynamic_slice_in_dim(sines, group * group_size, group_size, 0)[:, None, None, :]
        first = real_part[None] * cosine + imag_part[None] * sine
        second = imag_part[None] * cosine - real_part[None] * sine
        rotated = jnp.concatenate([first, second], axis=-1).astype(jnp.bfloat16)
        return jnp.einsum("gsbk,sak->gba", rotated, first_set, preferred_element_type=jnp.float32)

    result = lax.map(one_group, jnp.arange(lag_count // group_size, dtype=jnp.int32))
    return result.reshape(lag_count, second_set.shape[1], first_set.shape[1])


def general_device(traces, valid):
    length = traces.shape[2]
    dft_table, cosines, sines = make_tables(length, MAXLAG)
    whitened = whiten(traces, valid, dft_table)
    first_set = lax.all_gather(whitened, "col", axis=1, tiled=True)
    second_set = lax.all_gather(whitened, "row", axis=1, tiled=True)
    groups_row = lax.axis_size("row")
    seg_count = lax.axis_size("seg")
    segments_all = whitened.shape[0] * seg_count
    scale = 1.0 / math.sqrt(segments_all * (length // 2))
    own_count = whitened.shape[1]
    partial_value = lag_sums(first_set, second_set, cosines, sines, LAGSET)
    partial_value = partial_value.reshape(
        partial_value.shape[0], groups_row, own_count, partial_value.shape[2]
    )
    summed = lax.psum_scatter(partial_value, "seg", scatter_dimension=2, tiled=True)
    return summed * scale


def bin_order(length):
    return np.concatenate([np.arange(r, length // 2, 4) for r in range(4)])


def quarter_table(length):
    product = np.arange(length // 4)[:, None] * bin_order(length)[None, :] % length
    angle = 2.0 * np.pi / length * product
    return np.concatenate([np.cos(angle), -np.sin(angle)], axis=1).astype(jnp.bfloat16)


def lag_tables(length, max_shift, copies, rows):
    shifts = np.arange(2 * max_shift + 1) - max_shift
    product = shifts[:, None] * bin_order(length)[None, :] % length
    angle = 2.0 * np.pi / length * product
    out = []
    for table in (np.cos(angle), np.sin(angle)):
        full = np.zeros((rows, length // 2), np.float32)
        full[: copies * len(shifts)] = np.repeat(table, copies, axis=0)
        out.append(full)
    return out


def whiten_block(x_ref, v_ref, t_ref, w_ref):
    segs, own, length = x_ref.shape
    quarter, half = length // 4, length // 2
    rows, group = segs * own, half // 4
    stacked = jnp.concatenate(
        [x_ref[:, :, q * quarter : (q + 1) * quarter].reshape(rows, quarter) for q in range(4)],
        axis=0,
    )
    z = jnp.dot(stacked, t_ref[...], preferred_element_type=jnp.float32)

    def piece(q, r, imag):
        start = r * group + (half if imag else 0)
        return z[q * rows : (q + 1) * rows, start : start + group]

    real, imag = [], []
    for r in range(4):
        re, im = piece(0, r, False), piece(0, r, True)
        for q in range(1, 4):
            a, b = piece(q, r, False), piece(q, r, True)
            turn = (q * r) % 4
            if turn == 0:
                re, im = re + a, im + b
            elif turn == 1:
                re, im = re + b, im - a
            elif turn == 2:
                re, im = re - a, im - b
            else:
                re, im = re - b, im + a
        real.append(re)
        imag.append(im)
    power = [re * re + im * im for re, im in zip(real, imag)]
    level = jnp.sum(power[0] + power[1] + power[2] + power[3], axis=-1, keepdims=True) / half
    flags = v_ref[...].astype(jnp.float32)
    eye = lax.broadcasted_iota(jnp.int32, (own, own), 0) == lax.broadcasted_iota(
        jnp.int32, (own, own), 1
    )
    column = jnp.concatenate(
        [
            jnp.sum(
                jnp.where(eye, jnp.broadcast_to(flags[s : s + 1], (own, own)), 0.0),
                axis=-1,
                keepdims=True,
            )
            for s in range(segs)
        ],
        axis=0,
    )
    for r in range(4):
        factor = lax.rsqrt(power[r] + 0.1 * level + 1e-05) * column
        for base, part in ((0, real[r]), (half, imag[r])):
            value = (part * factor).astype(jnp.bfloat16).reshape(segs, own, group)
            w_ref[:, :, base + r * group : base + (r + 1) * group] = value


def whiten_own_kernel(
    x_in, v_in, t_in, c_in, s_in, w_ref, t_ref, c_out, s_out, x_ref, v_ref, sems
):
    pairs = ((x_in, x_ref), (t_in, t_ref), (v_in, v_ref), (c_in, c_out), (s_in, s_out))
    copies = [pltpu.make_async_copy(a, b, sems.at[i]) for i, (a, b) in enumerate(pairs)]
    for copy in copies:
        copy.start()
    for copy in copies[:3]:
        copy.wait()
    whiten_block(x_ref, v_ref, t_ref, w_ref)
    for copy in copies[3:]:
        copy.wait()


def rotate_kernel(seg_ref, w_ref, c_ref, s_ref, r_ref):
    segs, own, length = w_ref.shape
    half, part = length // 2, own // 2
    rows = c_ref.shape[0]
    first_half = seg_ref[0] == 0
    for seg in range(segs):
        w = w_ref[seg].astype(jnp.float32)
        low, high = w[:part], w[part:]
        keep = jnp.where(first_half, low, high)
        send = jnp.where(first_half, high, low)
        keep2 = jnp.concatenate([keep, keep], axis=0)
        send2 = jnp.concatenate([send, send], axis=0)
        for start in range(0, 2 * rows, 2 * own):
            pieces = []
            for row in (start, start + own):
                w2 = keep2 if row < rows else send2
                at = row % rows
                pieces.append((w2[:, :half], w2[:, half:], at))
            top, bottom = [], []
            for re, im, at in pieces:
                c, s = c_ref[at : at + own], s_ref[at : at + own]
                top.append(re * c + im * s)
                bottom.append(im * c - re * s)
            stop = start + 2 * own
            r_ref[seg, start:stop, :half] = jnp.concatenate(top, axis=0).astype(jnp.bfloat16)
            r_ref[seg, start:stop, half:] = jnp.concatenate(bottom, axis=0).astype(jnp.bfloat16)


def correlate_kernel(*refs):
    r_ref, keep_ref, send_ref = refs[0], refs[-2], refs[-1]
    blocks = refs[1:-2]
    rows = keep_ref.shape[0]
    total = None
    for seg in range(r_ref.shape[0]):
        first = []
        for at in range(0, len(blocks), 6):
            block, mate, pair_mate, pair, cross, cross_mate = blocks[at : at + 6]
            first += [block[seg], mate[seg], pair_mate[1, seg], pair_mate[0, seg]]
            first += [pair[0, seg], pair[1, seg], cross[seg], cross_mate[seg]]
        first = jnp.concatenate(first, axis=0)
        term = lax.dot_general(
            r_ref[seg], first, (((1,), (1,)), ((), ())), preferred_element_type=jnp.float32
        )
        total = term if total is None else total + term
    keep_ref[...] = total[:rows]
    send_ref[...] = total[rows:]


def pair_kernel(a_ref, b_ref, out_ref):
    out_ref[0] = a_ref[...]
    out_ref[1] = b_ref[...]


def finish_kernel(scale, own, me_ref, keep_ref, got_ref, out_ref):
    lags, part, lanes = out_ref.shape
    value = (keep_ref[: lags * part] + got_ref[: lags * part]) * scale
    lane = lax.broadcasted_iota(jnp.int32, value.shape, 1)
    low, high = (lane & (2 * own)) != 0, (lane & (4 * own)) != 0
    after, before = pltpu.roll(value, lanes - 2 * own, 1), pltpu.roll(value, 2 * own, 1)
    crossed = jnp.where(low & ~high, after, jnp.where(high & ~low, before, value))
    value = jnp.where((me_ref[0] & 1) != 0, crossed, value)
    width = own
    bit = 1
    while width < lanes:
        up = pltpu.roll(value, width, 1)
        down = pltpu.roll(value, lanes - width, 1)
        swapped = jnp.where((lane & width) != 0, up, down)
        value = jnp.where((me_ref[0] & bit) != 0, swapped, value)
        width, bit = 2 * width, 2 * bit
    for lag in range(lags):
        out_ref[lag] = value[lag * part : (lag + 1) * part]


CORE, SIDE, NEAR = 1, 2, 4


def far_blocks(col):
    held, steps = [0], []
    bit = col // 2
    while bit > NEAR:
        steps += [(m | bit, m, bit) for m in held]
        held += [m | bit for m in held]
        bit //= 2
    return held, steps


def hop(array, col, distance, other=None):
    other = distance if other is None else other
    return lax.ppermute(array, "col", [(i, i ^ (other if i & 1 else distance)) for i in range(col)])


def far_copies(traces, valid, col):
    raw = {0: (traces, valid)}
    for block, source, distance in far_blocks(col)[1]:
        far = hop(raw[source][0], col, distance)
        flag = hop(raw[source][1], col, distance)
        raw[block] = far, flag
    return raw


def spread(block, col):
    mate = hop(block, col, CORE)
    cross = hop(block, col, NEAR | SIDE)
    pair = pl.pallas_call(
        pair_kernel,
        out_shape=jax.ShapeDtypeStruct((2, *block.shape), block.dtype),
        in_specs=[VMEM] * 2,
        out_specs=VMEM,
        compiler_params=grant(2),
    )(block, mate)
    pair = hop(pair, col, NEAR, SIDE)
    pair_mate = hop(pair, col, CORE)
    cross_mate = hop(cross, col, CORE)
    return [block, mate, pair_mate, pair, cross, cross_mate]


def fast_device(traces, valid):
    return fast_body(traces, valid)


def fast_body(traces, valid):
    segs, own, length = traces.shape
    col = lax.axis_size("col")
    lags, part, lanes = 2 * MAXLAG + 1, own // 2, own * col
    half = length // 2
    rows = -(-lags * part // own) * own
    me = lax.axis_index("col").astype(jnp.int32).reshape(1)
    seg_index = lax.axis_index("seg").astype(jnp.int32).reshape(1)
    scale = 1.0 / math.sqrt(segs * lax.axis_size("seg") * half)

    table = quarter_table(length)
    lag_cos, lag_sin = lag_tables(length, MAXLAG, part, rows)
    raw = far_copies(traces, valid, col)
    whitened, table, cosines, sines = pl.pallas_call(
        whiten_own_kernel,
        out_shape=[
            jax.ShapeDtypeStruct(traces.shape, jnp.bfloat16),
            jax.ShapeDtypeStruct(table.shape, table.dtype),
            jax.ShapeDtypeStruct(lag_cos.shape, jnp.float32),
            jax.ShapeDtypeStruct(lag_sin.shape, jnp.float32),
        ],
        in_specs=[HBM] * 5,
        out_specs=[VMEM] * 4,
        scratch_shapes=[
            pltpu.VMEM(traces.shape, traces.dtype),
            pltpu.VMEM(valid.shape, valid.dtype),
            pltpu.SemaphoreType.DMA((5,)),
        ],
        compiler_params=grant(4),
    )(
        *[
            pltpu.with_memory_space_constraint(jnp.asarray(t), pltpu.HBM)
            for t in (traces, valid, table, lag_cos, lag_sin)
        ]
    )
    blocks = []
    for m, (far, flag) in raw.items():
        if m == 0:
            block = whitened
        else:
            block = pl.pallas_call(
                whiten_block,
                out_shape=jax.ShapeDtypeStruct(traces.shape, jnp.bfloat16),
                in_specs=[VMEM] * 3,
                out_specs=VMEM,
                compiler_params=grant(4),
            )(far, flag, table)
        blocks += spread(block, col)

    rotated = pl.pallas_call(
        rotate_kernel,
        out_shape=jax.ShapeDtypeStruct((segs, 2 * rows, length), jnp.bfloat16),
        in_specs=[SMEM, VMEM, VMEM, VMEM],
        out_specs=VMEM,
        compiler_params=grant(8),
        cost_estimate=pl.CostEstimate(
            flops=12 * segs * rows * length,
            bytes_accessed=4 * segs * rows * length,
            transcendentals=0,
        ),
    )(seg_index, whitened, cosines, sines)

    keep, send = pl.pallas_call(
        correlate_kernel,
        out_shape=[jax.ShapeDtypeStruct((rows, lanes), jnp.float32)] * 2,
        in_specs=[VMEM] * (1 + len(blocks)),
        out_specs=[VMEM] * 2,
        compiler_params=grant(12),
    )(rotated, *blocks)
    got = lax.ppermute(send, "seg", [(0, 1), (1, 0)])
    out = pl.pallas_call(
        functools.partial(finish_kernel, scale, own),
        out_shape=jax.ShapeDtypeStruct((lags, part, lanes), jnp.float32),
        in_specs=[SMEM, VMEM, VMEM],
        out_specs=VMEM,
        compiler_params=grant(2),
    )(me, keep, got)
    return out[:, None]


def on_device(traces, valid):
    fast = (
        fast_mesh(lax.axis_size("row"), lax.axis_size("col"), lax.axis_size("seg"))
        and traces.shape[1] == 8
        and traces.shape[1] * lax.axis_size("col") == 128
        and traces.shape[2] % 1024 == 0
    )
    return (fast_device if fast else general_device)(traces, valid)


def fast_mesh(row, col, seg):
    return row == 1 and seg == 2 and col >= 8 and col & (col - 1) == 0


def solution(mesh):
    placed = (P("seg", ("row", "col"), None), P("seg", ("row", "col")))
    return jax.shard_map(
        on_device,
        mesh=mesh,
        in_specs=placed,
        out_specs=P(None, None, ("col", "seg"), "row"),
        check_vma=False,
    )
```

```python
import functools
import math

import jax
import jax.numpy as jnp
import numpy as np
from jax import lax
from jax.experimental import pallas as pl
from jax.experimental.pallas import tpu as pltpu
from jax.sharding import PartitionSpec as P

MAXLAG = 16
LAGSET = 3
VMEM = pl.BlockSpec(memory_space=pltpu.VMEM)
SMEM = pl.BlockSpec(memory_space=pltpu.SMEM)
HBM = pl.BlockSpec(memory_space=pltpu.HBM)


def grant(mib):
    return pltpu.CompilerParams(vmem_limit_bytes=mib * 2**20)


def make_tables(length, max_shift):
    bins = jnp.arange(length // 2, dtype=jnp.int32)
    samples = jnp.arange(length, dtype=jnp.int32)
    product = samples[:, None] * bins[None, :] % length
    angle = 2.0 * math.pi / length * product.astype(jnp.float32)
    dft_table = jnp.concatenate([jnp.cos(angle), -jnp.sin(angle)], axis=1).astype(jnp.bfloat16)
    shifts = jnp.arange(2 * max_shift + 1, dtype=jnp.int32) - max_shift
    lag_prod = shifts[:, None] * bins[None, :] % length
    lag_angle = 2.0 * math.pi / length * lag_prod.astype(jnp.float32)
    return (dft_table, jnp.cos(lag_angle), jnp.sin(lag_angle))


def whiten(traces, valid, dft_table):
    length = traces.shape[2]
    half = length // 2
    flat = traces.reshape(-1, length)
    spectrum = jnp.dot(flat, dft_table, preferred_element_type=jnp.float32)
    spectrum = spectrum.reshape(traces.shape[0], traces.shape[1], length)
    real_part = spectrum[..., :half]
    imag_part = spectrum[..., half:]
    power = real_part * real_part + imag_part * imag_part
    level = jnp.mean(power, axis=-1, keepdims=True)
    factor = lax.rsqrt(power + 0.1 * level + 1e-05) * valid[..., None].astype(jnp.float32)
    return jnp.concatenate([real_part * factor, imag_part * factor], axis=-1).astype(jnp.bfloat16)


def lag_sums(first_set, second_set, cosines, sines, group_size):
    half = first_set.shape[2] // 2
    lag_count = cosines.shape[0]
    real_part = second_set[..., :half].astype(jnp.float32)
    imag_part = second_set[..., half:].astype(jnp.float32)

    def one_group(group):
        cosine = lax.dynamic_slice_in_dim(cosines, group * group_size, group_size, 0)[
            :, None, None, :
        ]
        sine = lax.dynamic_slice_in_dim(sines, group * group_size, group_size, 0)[:, None, None, :]
        first = real_part[None] * cosine + imag_part[None] * sine
        second = imag_part[None] * cosine - real_part[None] * sine
        rotated = jnp.concatenate([first, second], axis=-1).astype(jnp.bfloat16)
        return jnp.einsum("gsbk,sak->gba", rotated, first_set, preferred_element_type=jnp.float32)

    result = lax.map(one_group, jnp.arange(lag_count // group_size, dtype=jnp.int32))
    return result.reshape(lag_count, second_set.shape[1], first_set.shape[1])


def general_device(traces, valid):
    length = traces.shape[2]
    dft_table, cosines, sines = make_tables(length, MAXLAG)
    whitened = whiten(traces, valid, dft_table)
    first_set = lax.all_gather(whitened, "col", axis=1, tiled=True)
    second_set = lax.all_gather(whitened, "row", axis=1, tiled=True)
    groups_row = lax.axis_size("row")
    seg_count = lax.axis_size("seg")
    segments_all = whitened.shape[0] * seg_count
    scale = 1.0 / math.sqrt(segments_all * (length // 2))
    own_count = whitened.shape[1]
    partial_value = lag_sums(first_set, second_set, cosines, sines, LAGSET)
    partial_value = partial_value.reshape(
        partial_value.shape[0], groups_row, own_count, partial_value.shape[2]
    )
    summed = lax.psum_scatter(partial_value, "seg", scatter_dimension=2, tiled=True)
    return summed * scale


def bin_order(length):
    return np.concatenate([np.arange(r, length // 2, 4) for r in range(4)])


def quarter_table(length):
    product = np.arange(length // 4)[:, None] * bin_order(length)[None, :] % length
    angle = 2.0 * np.pi / length * product
    return np.concatenate([np.cos(angle), -np.sin(angle)], axis=1).astype(jnp.bfloat16)


def lag_tables(length, max_shift, copies, rows):
    shifts = np.arange(2 * max_shift + 1) - max_shift
    product = shifts[:, None] * bin_order(length)[None, :] % length
    angle = 2.0 * np.pi / length * product
    out = []
    for table in (np.cos(angle), np.sin(angle)):
        full = np.zeros((rows, length // 2), np.float32)
        full[: copies * len(shifts)] = np.repeat(table, copies, axis=0)
        out.append(full)
    return out


def whiten_kernel(
    x_in, v_in, t_in, c_in, s_in, w_ref, c_out, s_out, x_ref, v_ref, t_ref, sems
):
    pairs = ((x_in, x_ref), (t_in, t_ref), (v_in, v_ref), (c_in, c_out), (s_in, s_out))
    copies = [pltpu.make_async_copy(a, b, sems.at[i]) for i, (a, b) in enumerate(pairs)]
    for copy in copies:
        copy.start()
    segs, own, length = x_ref.shape
    for copy in copies[:3]:
        copy.wait()
    quarter, half = length // 4, length // 2
    rows, group = segs * own, half // 4
    stacked = jnp.concatenate(
        [x_ref[:, :, q * quarter : (q + 1) * quarter].reshape(rows, quarter) for q in range(4)],
        axis=0,
    )
    z = jnp.dot(stacked, t_ref[...], preferred_element_type=jnp.float32)

    def piece(q, r, imag):
        start = r * group + (half if imag else 0)
        return z[q * rows : (q + 1) * rows, start : start + group]

    real, imag = [], []
    for r in range(4):
        re, im = piece(0, r, False), piece(0, r, True)
        for q in range(1, 4):
            a, b = piece(q, r, False), piece(q, r, True)
            turn = (q * r) % 4
            if turn == 0:
                re, im = re + a, im + b
            elif turn == 1:
                re, im = re + b, im - a
            elif turn == 2:
                re, im = re - a, im - b
            else:
                re, im = re - b, im + a
        real.append(re)
        imag.append(im)
    power = [re * re + im * im for re, im in zip(real, imag)]
    level = jnp.sum(power[0] + power[1] + power[2] + power[3], axis=-1, keepdims=True) / half
    flags = v_ref[...].astype(jnp.float32)
    eye = lax.broadcasted_iota(jnp.int32, (own, own), 0) == lax.broadcasted_iota(
        jnp.int32, (own, own), 1
    )
    column = jnp.concatenate(
        [
            jnp.sum(
                jnp.where(eye, jnp.broadcast_to(flags[s : s + 1], (own, own)), 0.0),
                axis=-1,
                keepdims=True,
            )
            for s in range(segs)
        ],
        axis=0,
    )
    for r in range(4):
        factor = lax.rsqrt(power[r] + 0.1 * level + 1e-05) * column
        for base, part in ((0, real[r]), (half, imag[r])):
            value = (part * factor).astype(jnp.bfloat16).reshape(segs, own, group)
            w_ref[:, :, base + r * group : base + (r + 1) * group] = value
    for copy in copies[3:]:
        copy.wait()


def rotate_kernel(seg_ref, w_ref, c_ref, s_ref, r_ref):
    segs, own, length = w_ref.shape
    half, part = length // 2, own // 2
    rows = c_ref.shape[0]
    first_half = seg_ref[0] == 0
    for seg in range(segs):
        w = w_ref[seg].astype(jnp.float32)
        low, high = w[:part], w[part:]
        keep = jnp.where(first_half, low, high)
        send = jnp.where(first_half, high, low)
        keep2 = jnp.concatenate([keep, keep], axis=0)
        send2 = jnp.concatenate([send, send], axis=0)
        for start in range(0, 2 * rows, 2 * own):
            pieces = []
            for row in (start, start + own):
                w2 = keep2 if row < rows else send2
                at = row % rows
                pieces.append((w2[:, :half], w2[:, half:], at))
            top, bottom = [], []
            for re, im, at in pieces:
                c, s = c_ref[at : at + own], s_ref[at : at + own]
                top.append(re * c + im * s)
                bottom.append(im * c - re * s)
            stop = start + 2 * own
            r_ref[seg, start:stop, :half] = jnp.concatenate(top, axis=0).astype(jnp.bfloat16)
            r_ref[seg, start:stop, half:] = jnp.concatenate(bottom, axis=0).astype(jnp.bfloat16)


def products(r_ref, blocks, start, rows):
    total = None
    for seg in range(r_ref.shape[0]):
        block, mate, pair_mate, pair, cross, cross_mate = blocks[:6]
        first = [block[seg], mate[seg], pair_mate[1, seg], pair_mate[0, seg]]
        first += [pair[0, seg], pair[1, seg], cross[seg], cross_mate[seg]]
        first += [b[seg] for b in blocks[6:]]
        term = lax.dot_general(
            r_ref[seg, start : start + rows],
            jnp.concatenate(first, axis=0),
            (((1,), (1,)), ((), ())),
            preferred_element_type=jnp.float32,
        )
        total = term if total is None else total + term
    return total


def send_kernel(*refs):
    r_ref, blocks, send_ref = refs[0], refs[1:-1], refs[-1]
    rows = send_ref.shape[0]
    send_ref[...] = products(r_ref, blocks, rows, rows).astype(send_ref.dtype)


def keep_kernel(*refs):
    r_ref, blocks, keep_ref = refs[0], refs[1:-1], refs[-1]
    keep_ref[...] = products(r_ref, blocks, 0, keep_ref.shape[0])


def pair_kernel(a_ref, b_ref, out_ref):
    out_ref[0] = a_ref[...]
    out_ref[1] = b_ref[...]


def finish_kernel(scale, own, me_ref, keep_ref, got_ref, out_ref):
    lags, part, _ = out_ref.shape
    value = (keep_ref[...] + got_ref[...].astype(jnp.float32)) * scale
    lane = lax.broadcasted_iota(jnp.int32, value.shape, 1)
    me = me_ref[0]
    block = (lane // own) ^ me
    crossed = (block & ~6) | ((block & 2) << 1) | ((block & 4) >> 1)
    block = jnp.where(((me & 1) != 0) & (block < 8), crossed, block)
    value = jnp.take_along_axis(value, block * own + lane % own, axis=1)
    for lag in range(lags):
        out_ref[lag] = value[lag * part : (lag + 1) * part]


CORE, SIDE, NEAR = 1, 2, 4


def far_blocks(col):
    held, steps = [0], []
    bit = col // 2
    while bit > NEAR:
        steps += [(m | bit, m, bit) for m in held]
        held += [m | bit for m in held]
        bit //= 2
    return held, steps


def hop(array, col, distance, other=None):
    other = distance if other is None else other
    return lax.ppermute(array, "col", [(i, i ^ (other if i & 1 else distance)) for i in range(col)])


def gather(own_block, col):
    def swap(array):
        return hop(array, col, CORE)

    blocks = {0: own_block}
    held, steps = far_blocks(col)
    for block, source, distance in steps:
        blocks[block] = hop(blocks[source], col, distance)
    out = []
    for m in held:
        block = blocks[m]
        if m:
            parts = []
            for distance in (NEAR | SIDE, NEAR, SIDE):
                parts.append(hop(block, col, distance))
            cross, near, side = parts
            out += [block, swap(block), side, swap(side)]
            out += [near, swap(near), cross, swap(cross)]
            continue
        mate = swap(block)
        cross = hop(block, col, NEAR | SIDE)
        pair = pl.pallas_call(
            pair_kernel,
            out_shape=jax.ShapeDtypeStruct((2, *block.shape), block.dtype),
            in_specs=[VMEM] * 2,
            out_specs=VMEM,
            compiler_params=grant(2),
        )(block, mate)
        pair = hop(pair, col, NEAR, SIDE)
        out += [block, mate, swap(pair), pair, cross, swap(cross)]
    return out


def fast_device(traces, valid):
    return fast_body(traces, valid)


def fast_body(traces, valid):
    segs, own, length = traces.shape
    col = lax.axis_size("col")
    lags, part, lanes = 2 * MAXLAG + 1, own // 2, own * col
    half = length // 2
    rows = -(-lags * part // own) * own
    me = lax.axis_index("col").astype(jnp.int32).reshape(1)
    seg_index = lax.axis_index("seg").astype(jnp.int32).reshape(1)
    scale = 1.0 / math.sqrt(segs * lax.axis_size("seg") * half)

    table = quarter_table(length)
    lag_cos, lag_sin = lag_tables(length, MAXLAG, part, rows)
    whitened, cosines, sines = pl.pallas_call(
        whiten_kernel,
        out_shape=[
            jax.ShapeDtypeStruct(traces.shape, jnp.bfloat16),
            jax.ShapeDtypeStruct(lag_cos.shape, jnp.float32),
            jax.ShapeDtypeStruct(lag_sin.shape, jnp.float32),
        ],
        in_specs=[HBM] * 5,
        out_specs=[VMEM] * 3,
        scratch_shapes=[
            pltpu.VMEM(traces.shape, traces.dtype),
            pltpu.VMEM(valid.shape, valid.dtype),
            pltpu.VMEM(table.shape, table.dtype),
            pltpu.SemaphoreType.DMA((5,)),
        ],
        compiler_params=grant(4),
    )(
        *[
            pltpu.with_memory_space_constraint(jnp.asarray(t), pltpu.HBM)
            for t in (traces, valid, table, lag_cos, lag_sin)
        ]
    )

    blocks = gather(whitened, col)

    rotated = pl.pallas_call(
        rotate_kernel,
        out_shape=jax.ShapeDtypeStruct((segs, 2 * rows, length), jnp.bfloat16),
        in_specs=[SMEM, VMEM, VMEM, VMEM],
        out_specs=VMEM,
        compiler_params=grant(8),
        cost_estimate=pl.CostEstimate(
            flops=12 * segs * rows * length,
            bytes_accessed=4 * segs * rows * length,
            transcendentals=0,
        ),
    )(seg_index, whitened, cosines, sines)

    def multiply(kernel, dtype):
        return pl.pallas_call(
            kernel,
            out_shape=jax.ShapeDtypeStruct((rows, lanes), dtype),
            in_specs=[VMEM] * (1 + len(blocks)),
            out_specs=VMEM,
            compiler_params=grant(8),
            cost_estimate=pl.CostEstimate(
                flops=2 * rows * segs * length * lanes,
                bytes_accessed=2 * (rows + lanes) * segs * length,
                transcendentals=0,
            ),
        )(rotated, *blocks)

    send = multiply(send_kernel, jnp.bfloat16)
    got = lax.ppermute(send, "seg", [(0, 1), (1, 0)])
    keep = multiply(keep_kernel, jnp.float32)
    out = pl.pallas_call(
        functools.partial(finish_kernel, scale, own),
        out_shape=jax.ShapeDtypeStruct((lags, part, lanes), jnp.float32),
        in_specs=[SMEM, VMEM, VMEM],
        out_specs=VMEM,
        compiler_params=grant(2),
    )(me, keep, got)
    return out[:, None]


def on_device(traces, valid):
    fast = (
        fast_mesh(lax.axis_size("row"), lax.axis_size("col"), lax.axis_size("seg"))
        and traces.shape[1] == 8
        and traces.shape[1] * lax.axis_size("col") == 128
        and traces.shape[2] % 1024 == 0
    )
    return (fast_device if fast else general_device)(traces, valid)


def fast_mesh(row, col, seg):
    return row == 1 and seg == 2 and col >= 8 and col & (col - 1) == 0


def solution(mesh):
    placed = (P("seg", ("row", "col"), None), P("seg", ("row", "col")))
    return jax.shard_map(
        on_device,
        mesh=mesh,
        in_specs=placed,
        out_specs=P(None, None, ("col", "seg"), "row"),
        check_vma=False,
    )
```

```python
import functools
import math

import jax
import jax.numpy as jnp
import numpy as np
from jax import lax
from jax.experimental import pallas as pl
from jax.experimental.pallas import tpu as pltpu
from jax.sharding import PartitionSpec as P

MAXLAG = 16
LAGSET = 3
VMEM = pl.BlockSpec(memory_space=pltpu.VMEM)
SMEM = pl.BlockSpec(memory_space=pltpu.SMEM)
HBM = pl.BlockSpec(memory_space=pltpu.HBM)


def grant(mib):
    return pltpu.CompilerParams(vmem_limit_bytes=mib * 2**20)


def make_tables(length, max_shift):
    bins = jnp.arange(length // 2, dtype=jnp.int32)
    samples = jnp.arange(length, dtype=jnp.int32)
    product = samples[:, None] * bins[None, :] % length
    angle = 2.0 * math.pi / length * product.astype(jnp.float32)
    dft_table = jnp.concatenate([jnp.cos(angle), -jnp.sin(angle)], axis=1).astype(jnp.bfloat16)
    shifts = jnp.arange(2 * max_shift + 1, dtype=jnp.int32) - max_shift
    lag_prod = shifts[:, None] * bins[None, :] % length
    lag_angle = 2.0 * math.pi / length * lag_prod.astype(jnp.float32)
    return (dft_table, jnp.cos(lag_angle), jnp.sin(lag_angle))


def whiten(traces, valid, dft_table):
    length = traces.shape[2]
    half = length // 2
    flat = traces.reshape(-1, length)
    spectrum = jnp.dot(flat, dft_table, preferred_element_type=jnp.float32)
    spectrum = spectrum.reshape(traces.shape[0], traces.shape[1], length)
    real_part = spectrum[..., :half]
    imag_part = spectrum[..., half:]
    power = real_part * real_part + imag_part * imag_part
    level = jnp.mean(power, axis=-1, keepdims=True)
    factor = lax.rsqrt(power + 0.1 * level + 1e-05) * valid[..., None].astype(jnp.float32)
    return jnp.concatenate([real_part * factor, imag_part * factor], axis=-1).astype(jnp.bfloat16)


def lag_sums(first_set, second_set, cosines, sines, group_size):
    half = first_set.shape[2] // 2
    lag_count = cosines.shape[0]
    real_part = second_set[..., :half].astype(jnp.float32)
    imag_part = second_set[..., half:].astype(jnp.float32)

    def one_group(group):
        cosine = lax.dynamic_slice_in_dim(cosines, group * group_size, group_size, 0)[
            :, None, None, :
        ]
        sine = lax.dynamic_slice_in_dim(sines, group * group_size, group_size, 0)[:, None, None, :]
        first = real_part[None] * cosine + imag_part[None] * sine
        second = imag_part[None] * cosine - real_part[None] * sine
        rotated = jnp.concatenate([first, second], axis=-1).astype(jnp.bfloat16)
        return jnp.einsum("gsbk,sak->gba", rotated, first_set, preferred_element_type=jnp.float32)

    result = lax.map(one_group, jnp.arange(lag_count // group_size, dtype=jnp.int32))
    return result.reshape(lag_count, second_set.shape[1], first_set.shape[1])


def general_device(traces, valid):
    length = traces.shape[2]
    dft_table, cosines, sines = make_tables(length, MAXLAG)
    whitened = whiten(traces, valid, dft_table)
    first_set = lax.all_gather(whitened, "col", axis=1, tiled=True)
    second_set = lax.all_gather(whitened, "row", axis=1, tiled=True)
    groups_row = lax.axis_size("row")
    seg_count = lax.axis_size("seg")
    segments_all = whitened.shape[0] * seg_count
    scale = 1.0 / math.sqrt(segments_all * (length // 2))
    own_count = whitened.shape[1]
    partial_value = lag_sums(first_set, second_set, cosines, sines, LAGSET)
    partial_value = partial_value.reshape(
        partial_value.shape[0], groups_row, own_count, partial_value.shape[2]
    )
    summed = lax.psum_scatter(partial_value, "seg", scatter_dimension=2, tiled=True)
    return summed * scale


def bin_order(length):
    return np.concatenate([np.arange(r, length // 2, 4) for r in range(4)])


def lag_tables(length, max_shift, copies, rows):
    shifts = np.arange(2 * max_shift + 1) - max_shift
    product = shifts[:, None] * bin_order(length)[None, :] % length
    angle = 2.0 * np.pi / length * product
    out = []
    for table in (np.cos(angle), np.sin(angle)):
        full = np.zeros((rows, length // 2), np.float32)
        full[: copies * len(shifts)] = np.repeat(table, copies, axis=0)
        out.append(full)
    return out


def turn(index, length):
    quadrant = (index + length // 8) // (length // 4)
    angle = (index - quadrant * (length // 4)).astype(jnp.float32) * (2.0 * math.pi / length)
    square = angle * angle
    sine, cosine = 1.0 / 362880, 1.0 / 40320
    for top, bottom in ((-1.0 / 5040, -1.0 / 720), (1.0 / 120, 1.0 / 24), (-1.0 / 6, -0.5), (1.0, 1.0)):
        sine, cosine = sine * square + top, cosine * square + bottom
    sine = sine * angle
    odd = (quadrant & 1) != 0
    flip_sine = (quadrant & 2) != 0
    flip_cosine = ((quadrant + 1) & 2) != 0
    first, second = jnp.where(odd, sine, cosine), jnp.where(odd, cosine, sine)
    return jnp.where(flip_cosine, -first, first), jnp.where(flip_sine, -second, second)


def make_quarter_table(t_ref, e_ref):
    _, length = t_ref.shape
    half, coarse = length // 2, t_ref.shape[0] // 16
    column = lax.broadcasted_iota(jnp.int32, (16, half), 1)
    group = half // 4
    bins = 4 * (column % group) + column // group
    row = lax.broadcasted_iota(jnp.int32, (16, half), 0)
    fine_cos, fine_sin = turn(row * bins % length, length)
    for start in range(0, coarse, 16):
        cosine, sine = turn((row + start) * 16 * bins % length, length)
        e_ref[0, start : start + 16], e_ref[1, start : start + 16] = cosine, sine
    for i in range(coarse):
        cosine, sine = e_ref[0, i : i + 1], e_ref[1, i : i + 1]
        at = slice(16 * i, 16 * i + 16)
        t_ref[at, :half] = (cosine * fine_cos - sine * fine_sin).astype(t_ref.dtype)
        t_ref[at, half:] = (-(sine * fine_cos + cosine * fine_sin)).astype(t_ref.dtype)


def whiten_kernel(x_in, v_in, c_in, s_in, w_ref, c_out, s_out, x_ref, v_ref, t_ref, e_ref, sems):
    pairs = ((x_in, x_ref), (v_in, v_ref), (c_in, c_out), (s_in, s_out))
    copies = [pltpu.make_async_copy(a, b, sems.at[i]) for i, (a, b) in enumerate(pairs)]
    for copy in copies:
        copy.start()
    segs, own, length = x_ref.shape
    make_quarter_table(t_ref, e_ref)
    for copy in copies[:2]:
        copy.wait()
    quarter, half = length // 4, length // 2
    rows, group = segs * own, half // 4
    stacked = jnp.concatenate(
        [x_ref[:, :, q * quarter : (q + 1) * quarter].reshape(rows, quarter) for q in range(4)],
        axis=0,
    )
    z = jnp.dot(stacked, t_ref[...], preferred_element_type=jnp.float32)

    def piece(q, r, imag):
        start = r * group + (half if imag else 0)
        return z[q * rows : (q + 1) * rows, start : start + group]

    real, imag = [], []
    for r in range(4):
        re, im = piece(0, r, False), piece(0, r, True)
        for q in range(1, 4):
            a, b = piece(q, r, False), piece(q, r, True)
            turn = (q * r) % 4
            if turn == 0:
                re, im = re + a, im + b
            elif turn == 1:
                re, im = re + b, im - a
            elif turn == 2:
                re, im = re - a, im - b
            else:
                re, im = re - b, im + a
        real.append(re)
        imag.append(im)
    power = [re * re + im * im for re, im in zip(real, imag)]
    level = jnp.sum(power[0] + power[1] + power[2] + power[3], axis=-1, keepdims=True) / half
    flags = v_ref[...].astype(jnp.float32)
    eye = lax.broadcasted_iota(jnp.int32, (own, own), 0) == lax.broadcasted_iota(
        jnp.int32, (own, own), 1
    )
    column = jnp.concatenate(
        [
            jnp.sum(
                jnp.where(eye, jnp.broadcast_to(flags[s : s + 1], (own, own)), 0.0),
                axis=-1,
                keepdims=True,
            )
            for s in range(segs)
        ],
        axis=0,
    )
    for r in range(4):
        factor = lax.rsqrt(power[r] + 0.1 * level + 1e-05) * column
        for base, part in ((0, real[r]), (half, imag[r])):
            value = (part * factor).astype(jnp.bfloat16).reshape(segs, own, group)
            w_ref[:, :, base + r * group : base + (r + 1) * group] = value
    for copy in copies[2:]:
        copy.wait()


def rotate_kernel(seg_ref, w_ref, c_ref, s_ref, r_ref):
    segs, own, length = w_ref.shape
    half, part = length // 2, own // 2
    rows = c_ref.shape[0]
    first_half = seg_ref[0] == 0
    for seg in range(segs):
        w = w_ref[seg].astype(jnp.float32)
        low, high = w[:part], w[part:]
        keep = jnp.where(first_half, low, high)
        send = jnp.where(first_half, high, low)
        keep2 = jnp.concatenate([keep, keep], axis=0)
        send2 = jnp.concatenate([send, send], axis=0)
        for start in range(0, 2 * rows, 2 * own):
            pieces = []
            for row in (start, start + own):
                w2 = keep2 if row < rows else send2
                at = row % rows
                pieces.append((w2[:, :half], w2[:, half:], at))
            top, bottom = [], []
            for re, im, at in pieces:
                c, s = c_ref[at : at + own], s_ref[at : at + own]
                top.append(re * c + im * s)
                bottom.append(im * c - re * s)
            stop = start + 2 * own
            r_ref[seg, start:stop, :half] = jnp.concatenate(top, axis=0).astype(jnp.bfloat16)
            r_ref[seg, start:stop, half:] = jnp.concatenate(bottom, axis=0).astype(jnp.bfloat16)


def products(r_ref, blocks, start, rows):
    total = None
    for seg in range(r_ref.shape[0]):
        block, mate, pair_mate, pair, cross, cross_mate = blocks[:6]
        first = [block[seg], mate[seg], pair_mate[1, seg], pair_mate[0, seg]]
        first += [pair[0, seg], pair[1, seg], cross[seg], cross_mate[seg]]
        first += [b[seg] for b in blocks[6:]]
        term = lax.dot_general(
            r_ref[seg, start : start + rows],
            jnp.concatenate(first, axis=0),
            (((1,), (1,)), ((), ())),
            preferred_element_type=jnp.float32,
        )
        total = term if total is None else total + term
    return total


def send_kernel(*refs):
    r_ref, blocks, send_ref = refs[0], refs[1:-1], refs[-1]
    rows = send_ref.shape[0]
    send_ref[...] = products(r_ref, blocks, rows, rows).astype(send_ref.dtype)


def keep_kernel(*refs):
    r_ref, blocks, keep_ref = refs[0], refs[1:-1], refs[-1]
    keep_ref[...] = products(r_ref, blocks, 0, keep_ref.shape[0])


def pair_kernel(a_ref, b_ref, out_ref):
    out_ref[0] = a_ref[...]
    out_ref[1] = b_ref[...]


def finish_kernel(scale, own, me_ref, keep_ref, got_ref, out_ref):
    lags, part, _ = out_ref.shape
    value = (keep_ref[...] + got_ref[...].astype(jnp.float32)) * scale
    lane = lax.broadcasted_iota(jnp.int32, value.shape, 1)
    me = me_ref[0]
    block = (lane // own) ^ me
    crossed = (block & ~6) | ((block & 2) << 1) | ((block & 4) >> 1)
    block = jnp.where(((me & 1) != 0) & (block < 8), crossed, block)
    value = jnp.take_along_axis(value, block * own + lane % own, axis=1)
    for lag in range(lags):
        out_ref[lag] = value[lag * part : (lag + 1) * part]


CORE, SIDE, NEAR = 1, 2, 4


def far_blocks(col):
    held, steps = [0], []
    bit = col // 2
    while bit > NEAR:
        steps += [(m | bit, m, bit) for m in held]
        held += [m | bit for m in held]
        bit //= 2
    return held, steps


def hop(array, col, distance, other=None):
    other = distance if other is None else other
    return lax.ppermute(array, "col", [(i, i ^ (other if i & 1 else distance)) for i in range(col)])


def gather(own_block, col):
    def swap(array):
        return hop(array, col, CORE)

    blocks = {0: own_block}
    held, steps = far_blocks(col)
    for block, source, distance in steps:
        blocks[block] = hop(blocks[source], col, distance)
    out = []
    for m in held:
        block = blocks[m]
        if m:
            parts = []
            for distance in (NEAR | SIDE, NEAR, SIDE):
                parts.append(hop(block, col, distance))
            cross, near, side = parts
            out += [block, swap(block), side, swap(side)]
            out += [near, swap(near), cross, swap(cross)]
            continue
        mate = swap(block)
        cross = hop(block, col, NEAR | SIDE)
        pair = pl.pallas_call(
            pair_kernel,
            out_shape=jax.ShapeDtypeStruct((2, *block.shape), block.dtype),
            in_specs=[VMEM] * 2,
            out_specs=VMEM,
            compiler_params=grant(2),
        )(block, mate)
        pair = hop(pair, col, NEAR, SIDE)
        out += [block, mate, swap(pair), pair, cross, swap(cross)]
    return out


def fast_device(traces, valid):
    return fast_body(traces, valid)


def fast_body(traces, valid):
    segs, own, length = traces.shape
    col = lax.axis_size("col")
    lags, part, lanes = 2 * MAXLAG + 1, own // 2, own * col
    half = length // 2
    rows = -(-lags * part // own) * own
    me = lax.axis_index("col").astype(jnp.int32).reshape(1)
    seg_index = lax.axis_index("seg").astype(jnp.int32).reshape(1)
    scale = 1.0 / math.sqrt(segs * lax.axis_size("seg") * half)

    lag_cos, lag_sin = lag_tables(length, MAXLAG, part, rows)
    whitened, cosines, sines = pl.pallas_call(
        whiten_kernel,
        out_shape=[
            jax.ShapeDtypeStruct(traces.shape, jnp.bfloat16),
            jax.ShapeDtypeStruct(lag_cos.shape, jnp.float32),
            jax.ShapeDtypeStruct(lag_sin.shape, jnp.float32),
        ],
        in_specs=[HBM] * 4,
        out_specs=[VMEM] * 3,
        scratch_shapes=[
            pltpu.VMEM(traces.shape, traces.dtype),
            pltpu.VMEM(valid.shape, valid.dtype),
            pltpu.VMEM((length // 4, length), jnp.bfloat16),
            pltpu.VMEM((2, length // 64, half), jnp.float32),
            pltpu.SemaphoreType.DMA((4,)),
        ],
        compiler_params=grant(4),
    )(
        *[
            pltpu.with_memory_space_constraint(jnp.asarray(t), pltpu.HBM)
            for t in (traces, valid, lag_cos, lag_sin)
        ]
    )

    blocks = gather(whitened, col)

    rotated = pl.pallas_call(
        rotate_kernel,
        out_shape=jax.ShapeDtypeStruct((segs, 2 * rows, length), jnp.bfloat16),
        in_specs=[SMEM, VMEM, VMEM, VMEM],
        out_specs=VMEM,
        compiler_params=grant(8),
        cost_estimate=pl.CostEstimate(
            flops=12 * segs * rows * length,
            bytes_accessed=4 * segs * rows * length,
            transcendentals=0,
        ),
    )(seg_index, whitened, cosines, sines)

    def multiply(kernel, dtype):
        return pl.pallas_call(
            kernel,
            out_shape=jax.ShapeDtypeStruct((rows, lanes), dtype),
            in_specs=[VMEM] * (1 + len(blocks)),
            out_specs=VMEM,
            compiler_params=grant(8),
            cost_estimate=pl.CostEstimate(
                flops=2 * rows * segs * length * lanes,
                bytes_accessed=2 * (rows + lanes) * segs * length,
                transcendentals=0,
            ),
        )(rotated, *blocks)

    send = multiply(send_kernel, jnp.bfloat16)
    got = lax.ppermute(send, "seg", [(0, 1), (1, 0)])
    keep = multiply(keep_kernel, jnp.float32)
    out = pl.pallas_call(
        functools.partial(finish_kernel, scale, own),
        out_shape=jax.ShapeDtypeStruct((lags, part, lanes), jnp.float32),
        in_specs=[SMEM, VMEM, VMEM],
        out_specs=VMEM,
        compiler_params=grant(2),
    )(me, keep, got)
    return out[:, None]


def on_device(traces, valid):
    fast = (
        fast_mesh(lax.axis_size("row"), lax.axis_size("col"), lax.axis_size("seg"))
        and traces.shape[1] == 8
        and traces.shape[1] * lax.axis_size("col") == 128
        and traces.shape[2] % 1024 == 0
    )
    return (fast_device if fast else general_device)(traces, valid)


def fast_mesh(row, col, seg):
    return row == 1 and seg == 2 and col >= 8 and col & (col - 1) == 0


def solution(mesh):
    placed = (P("seg", ("row", "col"), None), P("seg", ("row", "col")))
    return jax.shard_map(
        on_device,
        mesh=mesh,
        in_specs=placed,
        out_specs=P(None, None, ("col", "seg"), "row"),
        check_vma=False,
    )
```

```python
import functools
import math

import jax
import jax.numpy as jnp
import numpy as np
from jax import lax
from jax.experimental import pallas as pl
from jax.experimental.pallas import tpu as pltpu
from jax.sharding import PartitionSpec as P

MAXLAG = 16
LAGSET = 3
VMEM = pl.BlockSpec(memory_space=pltpu.VMEM)
SMEM = pl.BlockSpec(memory_space=pltpu.SMEM)
HBM = pl.BlockSpec(memory_space=pltpu.HBM)


def grant(mib):
    return pltpu.CompilerParams(vmem_limit_bytes=mib * 2**20)


def make_tables(length, max_shift):
    bins = jnp.arange(length // 2, dtype=jnp.int32)
    samples = jnp.arange(length, dtype=jnp.int32)
    product = samples[:, None] * bins[None, :] % length
    angle = 2.0 * math.pi / length * product.astype(jnp.float32)
    dft_table = jnp.concatenate([jnp.cos(angle), -jnp.sin(angle)], axis=1).astype(jnp.bfloat16)
    shifts = jnp.arange(2 * max_shift + 1, dtype=jnp.int32) - max_shift
    lag_prod = shifts[:, None] * bins[None, :] % length
    lag_angle = 2.0 * math.pi / length * lag_prod.astype(jnp.float32)
    return (dft_table, jnp.cos(lag_angle), jnp.sin(lag_angle))


def whiten(traces, valid, dft_table):
    length = traces.shape[2]
    half = length // 2
    flat = traces.reshape(-1, length)
    spectrum = jnp.dot(flat, dft_table, preferred_element_type=jnp.float32)
    spectrum = spectrum.reshape(traces.shape[0], traces.shape[1], length)
    real_part = spectrum[..., :half]
    imag_part = spectrum[..., half:]
    power = real_part * real_part + imag_part * imag_part
    level = jnp.mean(power, axis=-1, keepdims=True)
    factor = lax.rsqrt(power + 0.1 * level + 1e-05) * valid[..., None].astype(jnp.float32)
    return jnp.concatenate([real_part * factor, imag_part * factor], axis=-1).astype(jnp.bfloat16)


def lag_sums(first_set, second_set, cosines, sines, group_size):
    half = first_set.shape[2] // 2
    lag_count = cosines.shape[0]
    real_part = second_set[..., :half].astype(jnp.float32)
    imag_part = second_set[..., half:].astype(jnp.float32)

    def one_group(group):
        cosine = lax.dynamic_slice_in_dim(cosines, group * group_size, group_size, 0)[
            :, None, None, :
        ]
        sine = lax.dynamic_slice_in_dim(sines, group * group_size, group_size, 0)[:, None, None, :]
        first = real_part[None] * cosine + imag_part[None] * sine
        second = imag_part[None] * cosine - real_part[None] * sine
        rotated = jnp.concatenate([first, second], axis=-1).astype(jnp.bfloat16)
        return jnp.einsum("gsbk,sak->gba", rotated, first_set, preferred_element_type=jnp.float32)

    result = lax.map(one_group, jnp.arange(lag_count // group_size, dtype=jnp.int32))
    return result.reshape(lag_count, second_set.shape[1], first_set.shape[1])


def general_device(traces, valid):
    length = traces.shape[2]
    dft_table, cosines, sines = make_tables(length, MAXLAG)
    whitened = whiten(traces, valid, dft_table)
    first_set = lax.all_gather(whitened, "col", axis=1, tiled=True)
    second_set = lax.all_gather(whitened, "row", axis=1, tiled=True)
    groups_row = lax.axis_size("row")
    seg_count = lax.axis_size("seg")
    segments_all = whitened.shape[0] * seg_count
    scale = 1.0 / math.sqrt(segments_all * (length // 2))
    own_count = whitened.shape[1]
    partial_value = lag_sums(first_set, second_set, cosines, sines, LAGSET)
    partial_value = partial_value.reshape(
        partial_value.shape[0], groups_row, own_count, partial_value.shape[2]
    )
    summed = lax.psum_scatter(partial_value, "seg", scatter_dimension=2, tiled=True)
    return summed * scale


def bin_order(length):
    return np.concatenate([np.arange(r, length // 2, 4) for r in range(4)])


def lag_tables(length, max_shift, copies, rows):
    shifts = np.arange(2 * max_shift + 1) - max_shift
    product = shifts[:, None] * bin_order(length)[None, :] % length
    angle = 2.0 * np.pi / length * product
    out = []
    for table in (np.cos(angle), np.sin(angle)):
        full = np.zeros((rows, length // 2), np.float32)
        full[: copies * len(shifts)] = np.repeat(table, copies, axis=0)
        out.append(full)
    return out


def turn(index, length):
    quadrant = (index + length // 8) // (length // 4)
    angle = (index - quadrant * (length // 4)).astype(jnp.float32) * (2.0 * math.pi / length)
    square = angle * angle
    sine, cosine = 1.0 / 362880, 1.0 / 40320
    for top, bottom in ((-1.0 / 5040, -1.0 / 720), (1.0 / 120, 1.0 / 24), (-1.0 / 6, -0.5), (1.0, 1.0)):
        sine, cosine = sine * square + top, cosine * square + bottom
    sine = sine * angle
    odd = (quadrant & 1) != 0
    flip_sine = (quadrant & 2) != 0
    flip_cosine = ((quadrant + 1) & 2) != 0
    first, second = jnp.where(odd, sine, cosine), jnp.where(odd, cosine, sine)
    return jnp.where(flip_cosine, -first, first), jnp.where(flip_sine, -second, second)


def make_quarter_table(t_ref, e_ref):
    _, length = t_ref.shape
    half, coarse = length // 2, t_ref.shape[0] // 16
    column = lax.broadcasted_iota(jnp.int32, (16, half), 1)
    group = half // 4
    bins = 4 * (column % group) + column // group
    row = lax.broadcasted_iota(jnp.int32, (16, half), 0)
    fine_cos, fine_sin = turn(row * bins % length, length)
    for start in range(0, coarse, 16):
        cosine, sine = turn((row + start) * 16 * bins % length, length)
        e_ref[0, start : start + 16], e_ref[1, start : start + 16] = cosine, sine
    for i in range(coarse):
        cosine, sine = e_ref[0, i : i + 1], e_ref[1, i : i + 1]
        at = slice(16 * i, 16 * i + 16)
        t_ref[at, :half] = (cosine * fine_cos - sine * fine_sin).astype(t_ref.dtype)
        t_ref[at, half:] = (-(sine * fine_cos + cosine * fine_sin)).astype(t_ref.dtype)


def whiten_kernel(x_in, v_in, c_in, s_in, w_ref, c_out, s_out, x_ref, v_ref, t_ref, e_ref, sems):
    pairs = ((x_in, x_ref), (v_in, v_ref), (c_in, c_out), (s_in, s_out))
    copies = [pltpu.make_async_copy(a, b, sems.at[i]) for i, (a, b) in enumerate(pairs)]
    segs, own, length = x_ref.shape
    parts = [
        pltpu.make_async_copy(x_in.at[i], x_ref.at[i], sems.at[len(pairs) + i]) for i in range(segs)
    ]
    for copy in parts + copies[1:]:
        copy.start()
    make_quarter_table(t_ref, e_ref)
    for copy in parts + copies[1:2]:
        copy.wait()
    quarter, half = length // 4, length // 2
    rows, group = segs * own, half // 4
    stacked = jnp.concatenate(
        [x_ref[:, :, q * quarter : (q + 1) * quarter].reshape(rows, quarter) for q in range(4)],
        axis=0,
    )
    z = jnp.dot(stacked, t_ref[...], preferred_element_type=jnp.float32)

    def piece(q, r, imag):
        start = r * group + (half if imag else 0)
        return z[q * rows : (q + 1) * rows, start : start + group]

    real, imag = [], []
    for r in range(4):
        re, im = piece(0, r, False), piece(0, r, True)
        for q in range(1, 4):
            a, b = piece(q, r, False), piece(q, r, True)
            turn = (q * r) % 4
            if turn == 0:
                re, im = re + a, im + b
            elif turn == 1:
                re, im = re + b, im - a
            elif turn == 2:
                re, im = re - a, im - b
            else:
                re, im = re - b, im + a
        real.append(re)
        imag.append(im)
    power = [re * re + im * im for re, im in zip(real, imag)]
    level = jnp.sum(power[0] + power[1] + power[2] + power[3], axis=-1, keepdims=True) / half
    flags = v_ref[...].astype(jnp.float32)
    eye = lax.broadcasted_iota(jnp.int32, (own, own), 0) == lax.broadcasted_iota(
        jnp.int32, (own, own), 1
    )
    column = jnp.concatenate(
        [
            jnp.sum(
                jnp.where(eye, jnp.broadcast_to(flags[s : s + 1], (own, own)), 0.0),
                axis=-1,
                keepdims=True,
            )
            for s in range(segs)
        ],
        axis=0,
    )
    for r in range(4):
        factor = lax.rsqrt(power[r] + 0.1 * level + 1e-05) * column
        for base, part in ((0, real[r]), (half, imag[r])):
            value = (part * factor).astype(jnp.bfloat16).reshape(segs, own, group)
            w_ref[:, :, base + r * group : base + (r + 1) * group] = value
    for copy in copies[2:]:
        copy.wait()


def rotate_kernel(seg_ref, w_ref, c_ref, s_ref, r_ref):
    segs, own, length = w_ref.shape
    half, part = length // 2, own // 2
    rows = c_ref.shape[0]
    first_half = seg_ref[0] == 0
    for seg in range(segs):
        w = w_ref[seg].astype(jnp.float32)
        low, high = w[:part], w[part:]
        keep = jnp.where(first_half, low, high)
        send = jnp.where(first_half, high, low)
        keep2 = jnp.concatenate([keep, keep], axis=0)
        send2 = jnp.concatenate([send, send], axis=0)
        for start in range(0, 2 * rows, 2 * own):
            pieces = []
            for row in (start, start + own):
                w2 = keep2 if row < rows else send2
                at = row % rows
                pieces.append((w2[:, :half], w2[:, half:], at))
            top, bottom = [], []
            for re, im, at in pieces:
                c, s = c_ref[at : at + own], s_ref[at : at + own]
                top.append(re * c + im * s)
                bottom.append(im * c - re * s)
            stop = start + 2 * own
            r_ref[seg, start:stop, :half] = jnp.concatenate(top, axis=0).astype(jnp.bfloat16)
            r_ref[seg, start:stop, half:] = jnp.concatenate(bottom, axis=0).astype(jnp.bfloat16)


def products(r_ref, blocks, start, rows):
    total = None
    for seg in range(r_ref.shape[0]):
        block, mate, pair_mate, pair, cross, cross_mate = blocks[:6]
        first = [block[seg], mate[seg], pair[0, seg], pair[1, seg]]
        first += [pair_mate[1, seg], pair_mate[0, seg], cross[seg], cross_mate[seg]]
        first += [b[seg] for b in blocks[6:]]
        term = lax.dot_general(
            r_ref[seg, start : start + rows],
            jnp.concatenate(first, axis=0),
            (((1,), (1,)), ((), ())),
            preferred_element_type=jnp.float32,
        )
        total = term if total is None else total + term
    return total


def send_kernel(*refs):
    r_ref, blocks, send_ref = refs[0], refs[1:-1], refs[-1]
    rows = send_ref.shape[0]
    send_ref[...] = products(r_ref, blocks, rows, rows).astype(send_ref.dtype)


def keep_kernel(*refs):
    r_ref, blocks, keep_ref = refs[0], refs[1:-1], refs[-1]
    keep_ref[...] = products(r_ref, blocks, 0, keep_ref.shape[0])


def pair_kernel(a_ref, b_ref, out_ref):
    out_ref[0] = a_ref[...]
    out_ref[1] = b_ref[...]


def finish_kernel(scale, own, me_ref, keep_ref, got_ref, out_ref):
    lags, part, _ = out_ref.shape
    value = (keep_ref[...] + got_ref[...].astype(jnp.float32)) * scale
    lane = lax.broadcasted_iota(jnp.int32, value.shape, 1)
    me = me_ref[0]
    block = (lane // own) ^ me
    crossed = (block & ~6) | ((block & 2) << 1) | ((block & 4) >> 1)
    block = jnp.where(((me & 1) != 0) & (block < 8), crossed, block)
    value = jnp.take_along_axis(value, block * own + lane % own, axis=1)
    for lag in range(lags):
        out_ref[lag] = value[lag * part : (lag + 1) * part]


CORE, SIDE, NEAR = 1, 2, 4


def far_blocks(col):
    held, steps = [0], []
    bit = col // 2
    while bit > NEAR:
        steps += [(m | bit, m, bit) for m in held]
        held += [m | bit for m in held]
        bit //= 2
    return held, steps


def hop(array, col, distance, other=None):
    other = distance if other is None else other
    return lax.ppermute(array, "col", [(i, i ^ (other if i & 1 else distance)) for i in range(col)])


def gather(own_block, col):
    def swap(array):
        return hop(array, col, CORE)

    blocks = {0: own_block}
    held, steps = far_blocks(col)
    for block, source, distance in steps:
        blocks[block] = hop(blocks[source], col, distance)
    out = []
    for m in held:
        block = blocks[m]
        if m:
            parts = []
            for name, distance in (("cross", m | NEAR | SIDE), ("near", NEAR), ("side", SIDE)):
                parts.append(hop(own_block if name == "cross" else block, col, distance))
            cross, near, side = parts
            out += [block, swap(block), side, swap(side)]
            out += [near, swap(near), cross, swap(cross)]
            continue
        mate = swap(block)
        cross = hop(block, col, NEAR | SIDE)
        pair = pl.pallas_call(
            pair_kernel,
            out_shape=jax.ShapeDtypeStruct((2, *block.shape), block.dtype),
            in_specs=[VMEM] * 2,
            out_specs=VMEM,
            compiler_params=grant(2),
        )(block, mate)
        pair = hop(pair, col, SIDE, NEAR)
        out += [block, mate, swap(pair), pair, cross, swap(cross)]
    return out


def fast_device(traces, valid):
    return fast_body(traces, valid)


def fast_body(traces, valid):
    segs, own, length = traces.shape
    col = lax.axis_size("col")
    lags, part, lanes = 2 * MAXLAG + 1, own // 2, own * col
    half = length // 2
    rows = -(-lags * part // own) * own
    me = lax.axis_index("col").astype(jnp.int32).reshape(1)
    seg_index = lax.axis_index("seg").astype(jnp.int32).reshape(1)
    scale = 1.0 / math.sqrt(segs * lax.axis_size("seg") * half)

    lag_cos, lag_sin = lag_tables(length, MAXLAG, part, rows)
    whitened, cosines, sines = pl.pallas_call(
        whiten_kernel,
        out_shape=[
            jax.ShapeDtypeStruct(traces.shape, jnp.bfloat16),
            jax.ShapeDtypeStruct(lag_cos.shape, jnp.float32),
            jax.ShapeDtypeStruct(lag_sin.shape, jnp.float32),
        ],
        in_specs=[HBM] * 4,
        out_specs=[VMEM] * 3,
        scratch_shapes=[
            pltpu.VMEM(traces.shape, traces.dtype),
            pltpu.VMEM(valid.shape, valid.dtype),
            pltpu.VMEM((length // 4, length), jnp.bfloat16),
            pltpu.VMEM((2, length // 64, half), jnp.float32),
            pltpu.SemaphoreType.DMA((4 + segs,)),
        ],
        compiler_params=grant(4),
    )(
        *[
            pltpu.with_memory_space_constraint(jnp.asarray(t), pltpu.HBM)
            for t in (traces, valid, lag_cos, lag_sin)
        ]
    )

    blocks = gather(whitened, col)

    rotated = pl.pallas_call(
        rotate_kernel,
        out_shape=jax.ShapeDtypeStruct((segs, 2 * rows, length), jnp.bfloat16),
        in_specs=[SMEM, VMEM, VMEM, VMEM],
        out_specs=VMEM,
        compiler_params=grant(8),
        cost_estimate=pl.CostEstimate(
            flops=12 * segs * rows * length,
            bytes_accessed=4 * segs * rows * length,
            transcendentals=0,
        ),
    )(seg_index, whitened, cosines, sines)

    def multiply(kernel, dtype):
        return pl.pallas_call(
            kernel,
            out_shape=jax.ShapeDtypeStruct((rows, lanes), dtype),
            in_specs=[VMEM] * (1 + len(blocks)),
            out_specs=VMEM,
            compiler_params=grant(8),
            cost_estimate=pl.CostEstimate(
                flops=2 * rows * segs * length * lanes,
                bytes_accessed=2 * (rows + lanes) * segs * length,
                transcendentals=0,
            ),
        )(rotated, *blocks)

    send = multiply(send_kernel, jnp.bfloat16)
    got = lax.ppermute(send, "seg", [(0, 1), (1, 0)])
    keep = multiply(keep_kernel, jnp.float32)
    out = pl.pallas_call(
        functools.partial(finish_kernel, scale, own),
        out_shape=jax.ShapeDtypeStruct((lags, part, lanes), jnp.float32),
        in_specs=[SMEM, VMEM, VMEM],
        out_specs=VMEM,
        compiler_params=grant(2),
    )(me, keep, got)
    return out[:, None]


def on_device(traces, valid):
    fast = (
        fast_mesh(lax.axis_size("row"), lax.axis_size("col"), lax.axis_size("seg"))
        and traces.shape[1] == 8
        and traces.shape[1] * lax.axis_size("col") == 128
        and traces.shape[2] % 1024 == 0
    )
    return (fast_device if fast else general_device)(traces, valid)


def fast_mesh(row, col, seg):
    return row == 1 and seg == 2 and col >= 8 and col & (col - 1) == 0


def solution(mesh):
    placed = (P("seg", ("row", "col"), None), P("seg", ("row", "col")))
    return jax.shard_map(
        on_device,
        mesh=mesh,
        in_specs=placed,
        out_specs=P(None, None, ("col", "seg"), "row"),
        check_vma=False,
    )
```

```python
import functools
import math

import jax
import jax.numpy as jnp
import numpy as np
from jax import lax
from jax.experimental import pallas as pl
from jax.experimental.pallas import tpu as pltpu
from jax.sharding import PartitionSpec as P

MAXLAG = 16
LAGSET = 3
VMEM = pl.BlockSpec(memory_space=pltpu.VMEM)
SMEM = pl.BlockSpec(memory_space=pltpu.SMEM)
HBM = pl.BlockSpec(memory_space=pltpu.HBM)


def grant(mib):
    return pltpu.CompilerParams(vmem_limit_bytes=mib * 2**20)


def make_tables(length, max_shift):
    bins = jnp.arange(length // 2, dtype=jnp.int32)
    samples = jnp.arange(length, dtype=jnp.int32)
    product = samples[:, None] * bins[None, :] % length
    angle = 2.0 * math.pi / length * product.astype(jnp.float32)
    dft_table = jnp.concatenate([jnp.cos(angle), -jnp.sin(angle)], axis=1).astype(jnp.bfloat16)
    shifts = jnp.arange(2 * max_shift + 1, dtype=jnp.int32) - max_shift
    lag_prod = shifts[:, None] * bins[None, :] % length
    lag_angle = 2.0 * math.pi / length * lag_prod.astype(jnp.float32)
    return (dft_table, jnp.cos(lag_angle), jnp.sin(lag_angle))


def whiten(traces, valid, dft_table):
    length = traces.shape[2]
    half = length // 2
    flat = traces.reshape(-1, length)
    spectrum = jnp.dot(flat, dft_table, preferred_element_type=jnp.float32)
    spectrum = spectrum.reshape(traces.shape[0], traces.shape[1], length)
    real_part = spectrum[..., :half]
    imag_part = spectrum[..., half:]
    power = real_part * real_part + imag_part * imag_part
    level = jnp.mean(power, axis=-1, keepdims=True)
    factor = lax.rsqrt(power + 0.1 * level + 1e-05) * valid[..., None].astype(jnp.float32)
    return jnp.concatenate([real_part * factor, imag_part * factor], axis=-1).astype(jnp.bfloat16)


def lag_sums(first_set, second_set, cosines, sines, group_size):
    half = first_set.shape[2] // 2
    lag_count = cosines.shape[0]
    real_part = second_set[..., :half].astype(jnp.float32)
    imag_part = second_set[..., half:].astype(jnp.float32)

    def one_group(group):
        cosine = lax.dynamic_slice_in_dim(cosines, group * group_size, group_size, 0)[
            :, None, None, :
        ]
        sine = lax.dynamic_slice_in_dim(sines, group * group_size, group_size, 0)[:, None, None, :]
        first = real_part[None] * cosine + imag_part[None] * sine
        second = imag_part[None] * cosine - real_part[None] * sine
        rotated = jnp.concatenate([first, second], axis=-1).astype(jnp.bfloat16)
        return jnp.einsum("gsbk,sak->gba", rotated, first_set, preferred_element_type=jnp.float32)

    result = lax.map(one_group, jnp.arange(lag_count // group_size, dtype=jnp.int32))
    return result.reshape(lag_count, second_set.shape[1], first_set.shape[1])


def general_device(traces, valid):
    length = traces.shape[2]
    dft_table, cosines, sines = make_tables(length, MAXLAG)
    whitened = whiten(traces, valid, dft_table)
    first_set = lax.all_gather(whitened, "col", axis=1, tiled=True)
    second_set = lax.all_gather(whitened, "row", axis=1, tiled=True)
    groups_row = lax.axis_size("row")
    seg_count = lax.axis_size("seg")
    segments_all = whitened.shape[0] * seg_count
    scale = 1.0 / math.sqrt(segments_all * (length // 2))
    own_count = whitened.shape[1]
    partial_value = lag_sums(first_set, second_set, cosines, sines, LAGSET)
    partial_value = partial_value.reshape(
        partial_value.shape[0], groups_row, own_count, partial_value.shape[2]
    )
    summed = lax.psum_scatter(partial_value, "seg", scatter_dimension=2, tiled=True)
    return summed * scale


def bin_order(length):
    return np.concatenate([np.arange(r, length // 2, 4) for r in range(4)])


def lag_tables(length, max_shift, copies, rows):
    shifts = np.arange(2 * max_shift + 1) - max_shift
    product = shifts[:, None] * bin_order(length)[None, :] % length
    angle = 2.0 * np.pi / length * product
    out = []
    for table in (np.cos(angle), np.sin(angle)):
        full = np.zeros((rows, length // 2), np.float32)
        full[: copies * len(shifts)] = np.repeat(table, copies, axis=0)
        out.append(full)
    return out


def turn(index, length):
    quadrant = (index + length // 8) // (length // 4)
    angle = (index - quadrant * (length // 4)).astype(jnp.float32) * (2.0 * math.pi / length)
    square = angle * angle
    sine, cosine = 1.0 / 362880, 1.0 / 40320
    for top, bottom in ((-1.0 / 5040, -1.0 / 720), (1.0 / 120, 1.0 / 24), (-1.0 / 6, -0.5), (1.0, 1.0)):
        sine, cosine = sine * square + top, cosine * square + bottom
    sine = sine * angle
    odd = (quadrant & 1) != 0
    flip_sine = (quadrant & 2) != 0
    flip_cosine = ((quadrant + 1) & 2) != 0
    first, second = jnp.where(odd, sine, cosine), jnp.where(odd, cosine, sine)
    return jnp.where(flip_cosine, -first, first), jnp.where(flip_sine, -second, second)


def make_quarter_table(t_ref, e_ref):
    _, length = t_ref.shape
    half, coarse = length // 2, t_ref.shape[0] // 16
    column = lax.broadcasted_iota(jnp.int32, (16, half), 1)
    group = half // 4
    bins = 4 * (column % group) + column // group
    row = lax.broadcasted_iota(jnp.int32, (16, half), 0)
    fine_cos, fine_sin = turn(row * bins % length, length)
    for start in range(0, coarse, 16):
        cosine, sine = turn((row + start) * 16 * bins % length, length)
        e_ref[0, start : start + 16], e_ref[1, start : start + 16] = cosine, sine
    for i in range(coarse):
        cosine, sine = e_ref[0, i : i + 1], e_ref[1, i : i + 1]
        at = slice(16 * i, 16 * i + 16)
        t_ref[at, :half] = (cosine * fine_cos - sine * fine_sin).astype(t_ref.dtype)
        t_ref[at, half:] = (-(sine * fine_cos + cosine * fine_sin)).astype(t_ref.dtype)


def whiten_kernel(x_in, v_in, c_in, s_in, w_ref, c_out, s_out, x_ref, v_ref, t_ref, e_ref, sems):
    pairs = ((x_in, x_ref), (v_in, v_ref), (c_in, c_out), (s_in, s_out))
    copies = [pltpu.make_async_copy(a, b, sems.at[i]) for i, (a, b) in enumerate(pairs)]
    for copy in copies:
        copy.start()
    segs, own, length = x_ref.shape
    make_quarter_table(t_ref, e_ref)
    for copy in copies[:2]:
        copy.wait()
    quarter, half = length // 4, length // 2
    rows, group = segs * own, half // 4
    stacked = jnp.concatenate(
        [x_ref[:, :, q * quarter : (q + 1) * quarter].reshape(rows, quarter) for q in range(4)],
        axis=0,
    )
    z = jnp.dot(stacked, t_ref[...], preferred_element_type=jnp.float32)

    def piece(q, r, imag):
        start = r * group + (half if imag else 0)
        return z[q * rows : (q + 1) * rows, start : start + group]

    real, imag = [], []
    for r in range(4):
        re, im = piece(0, r, False), piece(0, r, True)
        for q in range(1, 4):
            a, b = piece(q, r, False), piece(q, r, True)
            turn = (q * r) % 4
            if turn == 0:
                re, im = re + a, im + b
            elif turn == 1:
                re, im = re + b, im - a
            elif turn == 2:
                re, im = re - a, im - b
            else:
                re, im = re - b, im + a
        real.append(re)
        imag.append(im)
    power = [re * re + im * im for re, im in zip(real, imag)]
    level = jnp.sum(power[0] + power[1] + power[2] + power[3], axis=-1, keepdims=True) / half
    flags = v_ref[...].astype(jnp.float32)
    eye = lax.broadcasted_iota(jnp.int32, (own, own), 0) == lax.broadcasted_iota(
        jnp.int32, (own, own), 1
    )
    column = jnp.concatenate(
        [
            jnp.sum(
                jnp.where(eye, jnp.broadcast_to(flags[s : s + 1], (own, own)), 0.0),
                axis=-1,
                keepdims=True,
            )
            for s in range(segs)
        ],
        axis=0,
    )
    for r in range(4):
        factor = lax.rsqrt(power[r] + 0.1 * level + 1e-05) * column
        for base, part in ((0, real[r]), (half, imag[r])):
            value = (part * factor).astype(jnp.bfloat16).reshape(segs, own, group)
            w_ref[:, :, base + r * group : base + (r + 1) * group] = value
    for copy in copies[2:]:
        copy.wait()


def rotate_kernel(seg_ref, w_ref, c_ref, s_ref, r_ref):
    segs, own, length = w_ref.shape
    half, part = length // 2, own // 2
    rows = c_ref.shape[0]
    first_half = seg_ref[0] == 0
    for seg in range(segs):
        w = w_ref[seg].astype(jnp.float32)
        low, high = w[:part], w[part:]
        keep = jnp.where(first_half, low, high)
        send = jnp.where(first_half, high, low)
        keep2 = jnp.concatenate([keep, keep], axis=0)
        send2 = jnp.concatenate([send, send], axis=0)
        for start in range(0, 2 * rows, 2 * own):
            pieces = []
            for row in (start, start + own):
                w2 = keep2 if row < rows else send2
                at = row % rows
                pieces.append((w2[:, :half], w2[:, half:], at))
            top, bottom = [], []
            for re, im, at in pieces:
                c, s = c_ref[at : at + own], s_ref[at : at + own]
                top.append(re * c + im * s)
                bottom.append(im * c - re * s)
            stop = start + 2 * own
            r_ref[seg, start:stop, :half] = jnp.concatenate(top, axis=0).astype(jnp.bfloat16)
            r_ref[seg, start:stop, half:] = jnp.concatenate(bottom, axis=0).astype(jnp.bfloat16)


def products(r_ref, blocks, start, rows):
    total = None
    for seg in range(r_ref.shape[0]):
        term = lax.dot_general(
            r_ref[seg, start : start + rows],
            jnp.concatenate([block[seg] for block in blocks], axis=0),
            (((1,), (1,)), ((), ())),
            preferred_element_type=jnp.float32,
        )
        total = term if total is None else total + term
    return total


def send_kernel(*refs):
    r_ref, blocks, send_ref = refs[0], refs[1:-1], refs[-1]
    rows = send_ref.shape[0]
    send_ref[...] = products(r_ref, blocks, rows, rows).astype(send_ref.dtype)


def keep_kernel(*refs):
    r_ref, blocks, keep_ref = refs[0], refs[1:-1], refs[-1]
    keep_ref[...] = products(r_ref, blocks, 0, keep_ref.shape[0])


def finish_kernel(scale, own, me_ref, keep_ref, got_ref, out_ref):
    lags, part, _ = out_ref.shape
    value = (keep_ref[...] + got_ref[...].astype(jnp.float32)) * scale
    lane = lax.broadcasted_iota(jnp.int32, value.shape, 1)
    index = ((lane // own) ^ me_ref[0]) * own + lane % own
    value = jnp.take_along_axis(value, index, axis=1)
    for lag in range(lags):
        out_ref[lag] = value[lag * part : (lag + 1) * part]


CORE, SIDE, NEAR = 1, 2, 4


def gather_plan(col):
    cross = NEAR | SIDE
    held, plan = [0], []
    bit = col // 2
    while bit > NEAR:
        plan += [(m | bit, m, bit) for m in held]
        held += [m | bit for m in held]
        bit //= 2
    far = held[1:]
    plan += [(m | cross, 0, m | cross) for m in held]
    for m in held:
        plan += [(m | SIDE, m, SIDE), (m | NEAR, m, NEAR)]
    mates = [cross, 0, SIDE] + far + [NEAR]
    for m in far:
        mates += [m | cross, m | SIDE, m | NEAR]
    return plan + [(m | CORE, m, CORE) for m in mates]


def gather(own_block, col):
    blocks = {0: own_block}
    for block, source, distance in gather_plan(col):
        blocks[block] = lax.ppermute(blocks[source], "col", [(i, i ^ distance) for i in range(col)])
    return [blocks[m] for m in range(col)]


def fast_device(traces, valid):
    return fast_body(traces, valid)


def fast_body(traces, valid):
    segs, own, length = traces.shape
    col = lax.axis_size("col")
    lags, part, lanes = 2 * MAXLAG + 1, own // 2, own * col
    half = length // 2
    rows = -(-lags * part // own) * own
    me = lax.axis_index("col").astype(jnp.int32).reshape(1)
    seg_index = lax.axis_index("seg").astype(jnp.int32).reshape(1)
    scale = 1.0 / math.sqrt(segs * lax.axis_size("seg") * half)

    lag_cos, lag_sin = lag_tables(length, MAXLAG, part, rows)
    whitened, cosines, sines = pl.pallas_call(
        whiten_kernel,
        out_shape=[
            jax.ShapeDtypeStruct(traces.shape, jnp.bfloat16),
            jax.ShapeDtypeStruct(lag_cos.shape, jnp.float32),
            jax.ShapeDtypeStruct(lag_sin.shape, jnp.float32),
        ],
        in_specs=[HBM] * 4,
        out_specs=[VMEM] * 3,
        scratch_shapes=[
            pltpu.VMEM(traces.shape, traces.dtype),
            pltpu.VMEM(valid.shape, valid.dtype),
            pltpu.VMEM((length // 4, length), jnp.bfloat16),
            pltpu.VMEM((2, length // 64, half), jnp.float32),
            pltpu.SemaphoreType.DMA((4,)),
        ],
        compiler_params=grant(4),
    )(
        *[
            pltpu.with_memory_space_constraint(jnp.asarray(t), pltpu.HBM)
            for t in (traces, valid, lag_cos, lag_sin)
        ]
    )

    blocks = gather(whitened, col)

    rotated = pl.pallas_call(
        rotate_kernel,
        out_shape=jax.ShapeDtypeStruct((segs, 2 * rows, length), jnp.bfloat16),
        in_specs=[SMEM, VMEM, VMEM, VMEM],
        out_specs=VMEM,
        compiler_params=grant(8),
        cost_estimate=pl.CostEstimate(
            flops=12 * segs * rows * length,
            bytes_accessed=4 * segs * rows * length,
            transcendentals=0,
        ),
    )(seg_index, whitened, cosines, sines)

    def multiply(kernel, dtype):
        return pl.pallas_call(
            kernel,
            out_shape=jax.ShapeDtypeStruct((rows, lanes), dtype),
            in_specs=[VMEM] * (1 + len(blocks)),
            out_specs=VMEM,
            compiler_params=grant(8),
            cost_estimate=pl.CostEstimate(
                flops=2 * rows * segs * length * lanes,
                bytes_accessed=2 * (rows + lanes) * segs * length,
                transcendentals=0,
            ),
        )(pltpu.with_memory_space_constraint(rotated, pltpu.VMEM), *blocks)

    send = multiply(send_kernel, jnp.bfloat16)
    got = lax.ppermute(send, "seg", [(0, 1), (1, 0)])
    keep = multiply(keep_kernel, jnp.float32)
    out = pl.pallas_call(
        functools.partial(finish_kernel, scale, own),
        out_shape=jax.ShapeDtypeStruct((lags, part, lanes), jnp.float32),
        in_specs=[SMEM, VMEM, VMEM],
        out_specs=VMEM,
        compiler_params=grant(2),
    )(me, keep, got)
    return out[:, None]


def on_device(traces, valid):
    fast = (
        fast_mesh(lax.axis_size("row"), lax.axis_size("col"), lax.axis_size("seg"))
        and traces.shape[1] == 8
        and traces.shape[1] * lax.axis_size("col") == 128
        and traces.shape[2] % 1024 == 0
    )
    return (fast_device if fast else general_device)(traces, valid)


def fast_mesh(row, col, seg):
    return row == 1 and seg == 2 and col >= 8 and col & (col - 1) == 0


def solution(mesh):
    placed = (P("seg", ("row", "col"), None), P("seg", ("row", "col")))
    return jax.shard_map(
        on_device,
        mesh=mesh,
        in_specs=placed,
        out_specs=P(None, None, ("col", "seg"), "row"),
        check_vma=False,
    )
```

```python
import functools
import math

import jax
import jax.numpy as jnp
import numpy as np
from jax import lax
from jax.experimental import pallas as pl
from jax.experimental.pallas import tpu as pltpu
from jax.sharding import PartitionSpec as P

MAXLAG = 16
LAGSET = 3
VMEM = pl.BlockSpec(memory_space=pltpu.VMEM)
SMEM = pl.BlockSpec(memory_space=pltpu.SMEM)
HBM = pl.BlockSpec(memory_space=pltpu.HBM)


def grant(mib):
    return pltpu.CompilerParams(vmem_limit_bytes=mib * 2**20)


def make_tables(length, max_shift):
    bins = jnp.arange(length // 2, dtype=jnp.int32)
    samples = jnp.arange(length, dtype=jnp.int32)
    product = samples[:, None] * bins[None, :] % length
    angle = 2.0 * math.pi / length * product.astype(jnp.float32)
    dft_table = jnp.concatenate([jnp.cos(angle), -jnp.sin(angle)], axis=1).astype(jnp.bfloat16)
    shifts = jnp.arange(2 * max_shift + 1, dtype=jnp.int32) - max_shift
    lag_prod = shifts[:, None] * bins[None, :] % length
    lag_angle = 2.0 * math.pi / length * lag_prod.astype(jnp.float32)
    return (dft_table, jnp.cos(lag_angle), jnp.sin(lag_angle))


def whiten(traces, valid, dft_table):
    length = traces.shape[2]
    half = length // 2
    flat = traces.reshape(-1, length)
    spectrum = jnp.dot(flat, dft_table, preferred_element_type=jnp.float32)
    spectrum = spectrum.reshape(traces.shape[0], traces.shape[1], length)
    real_part = spectrum[..., :half]
    imag_part = spectrum[..., half:]
    power = real_part * real_part + imag_part * imag_part
    level = jnp.mean(power, axis=-1, keepdims=True)
    factor = lax.rsqrt(power + 0.1 * level + 1e-05) * valid[..., None].astype(jnp.float32)
    return jnp.concatenate([real_part * factor, imag_part * factor], axis=-1).astype(jnp.bfloat16)


def lag_sums(first_set, second_set, cosines, sines, group_size):
    half = first_set.shape[2] // 2
    lag_count = cosines.shape[0]
    real_part = second_set[..., :half].astype(jnp.float32)
    imag_part = second_set[..., half:].astype(jnp.float32)

    def one_group(group):
        cosine = lax.dynamic_slice_in_dim(cosines, group * group_size, group_size, 0)[
            :, None, None, :
        ]
        sine = lax.dynamic_slice_in_dim(sines, group * group_size, group_size, 0)[:, None, None, :]
        first = real_part[None] * cosine + imag_part[None] * sine
        second = imag_part[None] * cosine - real_part[None] * sine
        rotated = jnp.concatenate([first, second], axis=-1).astype(jnp.bfloat16)
        return jnp.einsum("gsbk,sak->gba", rotated, first_set, preferred_element_type=jnp.float32)

    result = lax.map(one_group, jnp.arange(lag_count // group_size, dtype=jnp.int32))
    return result.reshape(lag_count, second_set.shape[1], first_set.shape[1])


def general_device(traces, valid):
    length = traces.shape[2]
    dft_table, cosines, sines = make_tables(length, MAXLAG)
    whitened = whiten(traces, valid, dft_table)
    first_set = lax.all_gather(whitened, "col", axis=1, tiled=True)
    second_set = lax.all_gather(whitened, "row", axis=1, tiled=True)
    groups_row = lax.axis_size("row")
    seg_count = lax.axis_size("seg")
    segments_all = whitened.shape[0] * seg_count
    scale = 1.0 / math.sqrt(segments_all * (length // 2))
    own_count = whitened.shape[1]
    partial_value = lag_sums(first_set, second_set, cosines, sines, LAGSET)
    partial_value = partial_value.reshape(
        partial_value.shape[0], groups_row, own_count, partial_value.shape[2]
    )
    summed = lax.psum_scatter(partial_value, "seg", scatter_dimension=2, tiled=True)
    return summed * scale


def bin_order(length):
    return np.concatenate([np.arange(r, length // 2, 4) for r in range(4)])


def lag_tables(length, max_shift, copies, rows):
    shifts = np.arange(2 * max_shift + 1) - max_shift
    product = shifts[:, None] * bin_order(length)[None, :] % length
    angle = 2.0 * np.pi / length * product
    out = []
    for table in (np.cos(angle), np.sin(angle)):
        full = np.zeros((rows, length // 2), np.float32)
        full[: copies * len(shifts)] = np.repeat(table, copies, axis=0)
        out.append(full)
    return out


def turn(index, length):
    quadrant = (index + length // 8) // (length // 4)
    angle = (index - quadrant * (length // 4)).astype(jnp.float32) * (2.0 * math.pi / length)
    square = angle * angle
    sine, cosine = 1.0 / 362880, 1.0 / 40320
    for top, bottom in ((-1.0 / 5040, -1.0 / 720), (1.0 / 120, 1.0 / 24), (-1.0 / 6, -0.5), (1.0, 1.0)):
        sine, cosine = sine * square + top, cosine * square + bottom
    sine = sine * angle
    odd = (quadrant & 1) != 0
    flip_sine = (quadrant & 2) != 0
    flip_cosine = ((quadrant + 1) & 2) != 0
    first, second = jnp.where(odd, sine, cosine), jnp.where(odd, cosine, sine)
    return jnp.where(flip_cosine, -first, first), jnp.where(flip_sine, -second, second)


def make_quarter_table(t_ref, e_ref):
    _, length = t_ref.shape
    half, coarse = length // 2, t_ref.shape[0] // 16
    column = lax.broadcasted_iota(jnp.int32, (16, half), 1)
    group = half // 4
    bins = 4 * (column % group) + column // group
    row = lax.broadcasted_iota(jnp.int32, (16, half), 0)
    fine_cos, fine_sin = turn(row * bins % length, length)
    for start in range(0, coarse, 16):
        cosine, sine = turn((row + start) * 16 * bins % length, length)
        e_ref[0, start : start + 16], e_ref[1, start : start + 16] = cosine, sine
    for i in range(coarse):
        cosine, sine = e_ref[0, i : i + 1], e_ref[1, i : i + 1]
        at = slice(16 * i, 16 * i + 16)
        t_ref[at, :half] = (cosine * fine_cos - sine * fine_sin).astype(t_ref.dtype)
        t_ref[at, half:] = (-(sine * fine_cos + cosine * fine_sin)).astype(t_ref.dtype)


def whiten_kernel(x_in, v_in, c_in, s_in, w_ref, c_out, s_out, x_ref, v_ref, t_ref, e_ref, sems):
    pairs = ((x_in, x_ref), (v_in, v_ref), (c_in, c_out), (s_in, s_out))
    copies = [pltpu.make_async_copy(a, b, sems.at[i]) for i, (a, b) in enumerate(pairs)]
    for copy in copies:
        copy.start()
    segs, own, length = x_ref.shape
    make_quarter_table(t_ref, e_ref)
    for copy in copies[:2]:
        copy.wait()
    quarter, half = length // 4, length // 2
    rows, group = segs * own, half // 4
    stacked = jnp.concatenate(
        [x_ref[:, :, q * quarter : (q + 1) * quarter].reshape(rows, quarter) for q in range(4)],
        axis=0,
    )
    z = jnp.dot(stacked, t_ref[...], preferred_element_type=jnp.float32)

    def piece(q, r, imag):
        start = r * group + (half if imag else 0)
        return z[q * rows : (q + 1) * rows, start : start + group]

    real, imag = [], []
    for r in range(4):
        re, im = piece(0, r, False), piece(0, r, True)
        for q in range(1, 4):
            a, b = piece(q, r, False), piece(q, r, True)
            turn = (q * r) % 4
            if turn == 0:
                re, im = re + a, im + b
            elif turn == 1:
                re, im = re + b, im - a
            elif turn == 2:
                re, im = re - a, im - b
            else:
                re, im = re - b, im + a
        real.append(re)
        imag.append(im)
    power = [re * re + im * im for re, im in zip(real, imag)]
    level = jnp.sum(power[0] + power[1] + power[2] + power[3], axis=-1, keepdims=True) / half
    flags = v_ref[...].astype(jnp.float32)
    eye = lax.broadcasted_iota(jnp.int32, (own, own), 0) == lax.broadcasted_iota(
        jnp.int32, (own, own), 1
    )
    column = jnp.concatenate(
        [
            jnp.sum(
                jnp.where(eye, jnp.broadcast_to(flags[s : s + 1], (own, own)), 0.0),
                axis=-1,
                keepdims=True,
            )
            for s in range(segs)
        ],
        axis=0,
    )
    for r in range(4):
        factor = lax.rsqrt(power[r] + 0.1 * level + 1e-05) * column
        for base, part in ((0, real[r]), (half, imag[r])):
            value = (part * factor).astype(jnp.bfloat16).reshape(segs, own, group)
            w_ref[:, :, base + r * group : base + (r + 1) * group] = value
    for copy in copies[2:]:
        copy.wait()


def rotate_kernel(seg_ref, w_ref, c_ref, s_ref, r_ref):
    segs, own, length = w_ref.shape
    half, part = length // 2, own // 2
    rows = c_ref.shape[0]
    first_half = seg_ref[0] == 0
    for seg in range(segs):
        w = w_ref[seg].astype(jnp.float32)
        low, high = w[:part], w[part:]
        keep = jnp.where(first_half, low, high)
        send = jnp.where(first_half, high, low)
        keep2 = jnp.concatenate([keep, keep], axis=0)
        send2 = jnp.concatenate([send, send], axis=0)
        for start in range(0, 2 * rows, 2 * own):
            pieces = []
            for row in (start, start + own):
                w2 = keep2 if row < rows else send2
                at = row % rows
                pieces.append((w2[:, :half], w2[:, half:], at))
            top, bottom = [], []
            for re, im, at in pieces:
                c, s = c_ref[at : at + own], s_ref[at : at + own]
                top.append(re * c + im * s)
                bottom.append(im * c - re * s)
            stop = start + 2 * own
            r_ref[seg, start:stop, :half] = jnp.concatenate(top, axis=0).astype(jnp.bfloat16)
            r_ref[seg, start:stop, half:] = jnp.concatenate(bottom, axis=0).astype(jnp.bfloat16)


def products(r_ref, blocks, start, rows):
    total = None
    for seg in range(r_ref.shape[0]):
        term = lax.dot_general(
            r_ref[seg, start : start + rows],
            jnp.concatenate([block[seg] for block in blocks], axis=0),
            (((1,), (1,)), ((), ())),
            preferred_element_type=jnp.float32,
        )
        total = term if total is None else total + term
    return total


def send_kernel(*refs):
    r_ref, blocks, send_ref = refs[0], refs[1:-1], refs[-1]
    rows = send_ref.shape[0]
    send_ref[...] = products(r_ref, blocks, rows, rows).astype(send_ref.dtype)


def keep_kernel(*refs):
    r_ref, blocks, keep_ref = refs[0], refs[1:-1], refs[-1]
    keep_ref[...] = products(r_ref, blocks, 0, keep_ref.shape[0])


def finish_kernel(scale, own, me_ref, keep_ref, got_ref, out_ref):
    lags, part, _ = out_ref.shape
    value = (keep_ref[...] + got_ref[...].astype(jnp.float32)) * scale
    lane = lax.broadcasted_iota(jnp.int32, value.shape, 1)
    me = me_ref[0]
    block = (lane // own) ^ me
    crossed = (block & ~6) | ((block & 2) << 1) | ((block & 4) >> 1)
    block = jnp.where((me & 1) != 0, crossed, block)
    index = block * own + lane % own
    value = jnp.take_along_axis(value, index, axis=1)
    for lag in range(lags):
        out_ref[lag] = value[lag * part : (lag + 1) * part]


CORE, SIDE, NEAR = 1, 2, 4


def gather_plan(col):
    cross = NEAR | SIDE
    held, plan = [0], []
    bit = col // 2
    while bit > NEAR:
        plan += [(m | bit, m, bit, bit) for m in held]
        held += [m | bit for m in held]
        bit //= 2
    far = held[1:]
    plan += [(m | cross, 0, m | cross, m | cross) for m in held]
    for m in held:
        plan += [(m | SIDE, m, SIDE, NEAR), (m | NEAR, m, NEAR, SIDE)]
    mates = [0, cross] + far + [SIDE, NEAR]
    for m in far:
        mates += [m | SIDE, m | cross, m | NEAR]
    return plan + [(m | CORE, m, CORE, CORE) for m in mates]


def gather(own_block, col):
    blocks = {0: own_block}
    for block, source, even, odd in gather_plan(col):
        pairs = [(i, i ^ (odd if i & 1 else even)) for i in range(col)]
        blocks[block] = lax.ppermute(blocks[source], "col", pairs)
    order = [m ^ (6 if m & 1 and (m & 6) in (SIDE, NEAR) else 0) for m in range(col)]
    return [blocks[m] for m in order]


def fast_device(traces, valid):
    return fast_body(traces, valid)


def fast_body(traces, valid):
    segs, own, length = traces.shape
    col = lax.axis_size("col")
    lags, part, lanes = 2 * MAXLAG + 1, own // 2, own * col
    half = length // 2
    rows = -(-lags * part // own) * own
    me = lax.axis_index("col").astype(jnp.int32).reshape(1)
    seg_index = lax.axis_index("seg").astype(jnp.int32).reshape(1)
    scale = 1.0 / math.sqrt(segs * lax.axis_size("seg") * half)

    lag_cos, lag_sin = lag_tables(length, MAXLAG, part, rows)
    whitened, cosines, sines = pl.pallas_call(
        whiten_kernel,
        out_shape=[
            jax.ShapeDtypeStruct(traces.shape, jnp.bfloat16),
            jax.ShapeDtypeStruct(lag_cos.shape, jnp.float32),
            jax.ShapeDtypeStruct(lag_sin.shape, jnp.float32),
        ],
        in_specs=[HBM] * 4,
        out_specs=[VMEM] * 3,
        scratch_shapes=[
            pltpu.VMEM(traces.shape, traces.dtype),
            pltpu.VMEM(valid.shape, valid.dtype),
            pltpu.VMEM((length // 4, length), jnp.bfloat16),
            pltpu.VMEM((2, length // 64, half), jnp.float32),
            pltpu.SemaphoreType.DMA((4,)),
        ],
        compiler_params=grant(4),
    )(
        *[
            pltpu.with_memory_space_constraint(jnp.asarray(t), pltpu.HBM)
            for t in (traces, valid, lag_cos, lag_sin)
        ]
    )

    blocks = gather(whitened, col)

    rotated = pl.pallas_call(
        rotate_kernel,
        out_shape=jax.ShapeDtypeStruct((segs, 2 * rows, length), jnp.bfloat16),
        in_specs=[SMEM, VMEM, VMEM, VMEM],
        out_specs=VMEM,
        compiler_params=grant(8),
        cost_estimate=pl.CostEstimate(
            flops=12 * segs * rows * length,
            bytes_accessed=4 * segs * rows * length,
            transcendentals=0,
        ),
    )(seg_index, whitened, cosines, sines)

    def multiply(kernel, dtype):
        return pl.pallas_call(
            kernel,
            out_shape=jax.ShapeDtypeStruct((rows, lanes), dtype),
            in_specs=[VMEM] * (1 + len(blocks)),
            out_specs=VMEM,
            compiler_params=grant(8),
            cost_estimate=pl.CostEstimate(
                flops=2 * rows * segs * length * lanes,
                bytes_accessed=2 * (rows + lanes) * segs * length,
                transcendentals=0,
            ),
        )(*[pltpu.with_memory_space_constraint(x, pltpu.VMEM) for x in (rotated, *blocks)])

    send = multiply(send_kernel, jnp.bfloat16)
    got = lax.ppermute(send, "seg", [(0, 1), (1, 0)])
    keep = multiply(keep_kernel, jnp.float32)
    out = pl.pallas_call(
        functools.partial(finish_kernel, scale, own),
        out_shape=jax.ShapeDtypeStruct((lags, part, lanes), jnp.float32),
        in_specs=[SMEM, VMEM, VMEM],
        out_specs=VMEM,
        compiler_params=grant(2),
    )(me, keep, got)
    return out[:, None]


def on_device(traces, valid):
    fast = (
        fast_mesh(lax.axis_size("row"), lax.axis_size("col"), lax.axis_size("seg"))
        and traces.shape[1] == 8
        and traces.shape[1] * lax.axis_size("col") == 128
        and traces.shape[2] % 1024 == 0
    )
    return (fast_device if fast else general_device)(traces, valid)


def fast_mesh(row, col, seg):
    return row == 1 and seg == 2 and col >= 8 and col & (col - 1) == 0


def solution(mesh):
    placed = (P("seg", ("row", "col"), None), P("seg", ("row", "col")))
    return jax.shard_map(
        on_device,
        mesh=mesh,
        in_specs=placed,
        out_specs=P(None, None, ("col", "seg"), "row"),
        check_vma=False,
    )
```

```python
import functools
import math

import jax
import jax.numpy as jnp
import numpy as np
from jax import lax
from jax.experimental import pallas as pl
from jax.experimental.pallas import tpu as pltpu
from jax.sharding import PartitionSpec as P

MAXLAG = 16
LAGSET = 3
VMEM = pl.BlockSpec(memory_space=pltpu.VMEM)
SMEM = pl.BlockSpec(memory_space=pltpu.SMEM)
HBM = pl.BlockSpec(memory_space=pltpu.HBM)


def grant(mib):
    return pltpu.CompilerParams(vmem_limit_bytes=mib * 2**20)


def make_tables(length, max_shift):
    bins = jnp.arange(length // 2, dtype=jnp.int32)
    samples = jnp.arange(length, dtype=jnp.int32)
    product = samples[:, None] * bins[None, :] % length
    angle = 2.0 * math.pi / length * product.astype(jnp.float32)
    dft_table = jnp.concatenate([jnp.cos(angle), -jnp.sin(angle)], axis=1).astype(jnp.bfloat16)
    shifts = jnp.arange(2 * max_shift + 1, dtype=jnp.int32) - max_shift
    lag_prod = shifts[:, None] * bins[None, :] % length
    lag_angle = 2.0 * math.pi / length * lag_prod.astype(jnp.float32)
    return (dft_table, jnp.cos(lag_angle), jnp.sin(lag_angle))


def whiten(traces, valid, dft_table):
    length = traces.shape[2]
    half = length // 2
    flat = traces.reshape(-1, length)
    spectrum = jnp.dot(flat, dft_table, preferred_element_type=jnp.float32)
    spectrum = spectrum.reshape(traces.shape[0], traces.shape[1], length)
    real_part = spectrum[..., :half]
    imag_part = spectrum[..., half:]
    power = real_part * real_part + imag_part * imag_part
    level = jnp.mean(power, axis=-1, keepdims=True)
    factor = lax.rsqrt(power + 0.1 * level + 1e-05) * valid[..., None].astype(jnp.float32)
    return jnp.concatenate([real_part * factor, imag_part * factor], axis=-1).astype(jnp.bfloat16)


def lag_sums(first_set, second_set, cosines, sines, group_size):
    half = first_set.shape[2] // 2
    lag_count = cosines.shape[0]
    real_part = second_set[..., :half].astype(jnp.float32)
    imag_part = second_set[..., half:].astype(jnp.float32)

    def one_group(group):
        cosine = lax.dynamic_slice_in_dim(cosines, group * group_size, group_size, 0)[
            :, None, None, :
        ]
        sine = lax.dynamic_slice_in_dim(sines, group * group_size, group_size, 0)[:, None, None, :]
        first = real_part[None] * cosine + imag_part[None] * sine
        second = imag_part[None] * cosine - real_part[None] * sine
        rotated = jnp.concatenate([first, second], axis=-1).astype(jnp.bfloat16)
        return jnp.einsum("gsbk,sak->gba", rotated, first_set, preferred_element_type=jnp.float32)

    result = lax.map(one_group, jnp.arange(lag_count // group_size, dtype=jnp.int32))
    return result.reshape(lag_count, second_set.shape[1], first_set.shape[1])


def general_device(traces, valid):
    length = traces.shape[2]
    dft_table, cosines, sines = make_tables(length, MAXLAG)
    whitened = whiten(traces, valid, dft_table)
    first_set = lax.all_gather(whitened, "col", axis=1, tiled=True)
    second_set = lax.all_gather(whitened, "row", axis=1, tiled=True)
    groups_row = lax.axis_size("row")
    seg_count = lax.axis_size("seg")
    segments_all = whitened.shape[0] * seg_count
    scale = 1.0 / math.sqrt(segments_all * (length // 2))
    own_count = whitened.shape[1]
    partial_value = lag_sums(first_set, second_set, cosines, sines, LAGSET)
    partial_value = partial_value.reshape(
        partial_value.shape[0], groups_row, own_count, partial_value.shape[2]
    )
    summed = lax.psum_scatter(partial_value, "seg", scatter_dimension=2, tiled=True)
    return summed * scale


def bin_order(length):
    return np.concatenate([np.arange(r, length // 2, 4) for r in range(4)])


def lag_tables(length, max_shift, copies, rows):
    shifts = np.arange(2 * max_shift + 1) - max_shift
    product = shifts[:, None] * bin_order(length)[None, :] % length
    angle = 2.0 * np.pi / length * product
    out = []
    for table in (np.cos(angle), np.sin(angle)):
        full = np.zeros((rows, length // 2), np.float32)
        full[: copies * len(shifts)] = np.repeat(table, copies, axis=0)
        out.append(full)
    return out


def turn(index, length):
    quadrant = (index + length // 8) // (length // 4)
    angle = (index - quadrant * (length // 4)).astype(jnp.float32) * (2.0 * math.pi / length)
    square = angle * angle
    sine, cosine = 1.0 / 362880, 1.0 / 40320
    for top, bottom in ((-1.0 / 5040, -1.0 / 720), (1.0 / 120, 1.0 / 24), (-1.0 / 6, -0.5), (1.0, 1.0)):
        sine, cosine = sine * square + top, cosine * square + bottom
    sine = sine * angle
    odd = (quadrant & 1) != 0
    flip_sine = (quadrant & 2) != 0
    flip_cosine = ((quadrant + 1) & 2) != 0
    first, second = jnp.where(odd, sine, cosine), jnp.where(odd, cosine, sine)
    return jnp.where(flip_cosine, -first, first), jnp.where(flip_sine, -second, second)


def make_quarter_table(t_ref, e_ref):
    _, length = t_ref.shape
    half, coarse = length // 2, t_ref.shape[0] // 16
    column = lax.broadcasted_iota(jnp.int32, (16, half), 1)
    group = half // 4
    bins = 4 * (column % group) + column // group
    row = lax.broadcasted_iota(jnp.int32, (16, half), 0)
    fine_cos, fine_sin = turn(row * bins % length, length)
    for start in range(0, coarse, 16):
        cosine, sine = turn((row + start) * 16 * bins % length, length)
        e_ref[0, start : start + 16], e_ref[1, start : start + 16] = cosine, sine
    for i in range(coarse):
        cosine, sine = e_ref[0, i : i + 1], e_ref[1, i : i + 1]
        at = slice(16 * i, 16 * i + 16)
        t_ref[at, :half] = (cosine * fine_cos - sine * fine_sin).astype(t_ref.dtype)
        t_ref[at, half:] = (-(sine * fine_cos + cosine * fine_sin)).astype(t_ref.dtype)


def whiten_kernel(x_in, v_in, c_in, s_in, w_ref, c_out, s_out, x_ref, v_ref, t_ref, e_ref, sems):
    pairs = ((x_in, x_ref), (v_in, v_ref), (c_in, c_out), (s_in, s_out))
    copies = [pltpu.make_async_copy(a, b, sems.at[i]) for i, (a, b) in enumerate(pairs)]
    for copy in copies:
        copy.start()
    segs, own, length = x_ref.shape
    make_quarter_table(t_ref, e_ref)
    for copy in copies[:2]:
        copy.wait()
    quarter, half = length // 4, length // 2
    rows, group = segs * own, half // 4
    stacked = jnp.concatenate(
        [x_ref[:, :, q * quarter : (q + 1) * quarter].reshape(rows, quarter) for q in range(4)],
        axis=0,
    )
    z = jnp.dot(stacked, t_ref[...], preferred_element_type=jnp.float32)

    def piece(q, r, imag):
        start = r * group + (half if imag else 0)
        return z[q * rows : (q + 1) * rows, start : start + group]

    real, imag = [], []
    for r in range(4):
        re, im = piece(0, r, False), piece(0, r, True)
        for q in range(1, 4):
            a, b = piece(q, r, False), piece(q, r, True)
            turn = (q * r) % 4
            if turn == 0:
                re, im = re + a, im + b
            elif turn == 1:
                re, im = re + b, im - a
            elif turn == 2:
                re, im = re - a, im - b
            else:
                re, im = re - b, im + a
        real.append(re)
        imag.append(im)
    power = [re * re + im * im for re, im in zip(real, imag)]
    level = jnp.sum(power[0] + power[1] + power[2] + power[3], axis=-1, keepdims=True) / half
    flags = v_ref[...].astype(jnp.float32)
    eye = lax.broadcasted_iota(jnp.int32, (own, own), 0) == lax.broadcasted_iota(
        jnp.int32, (own, own), 1
    )
    column = jnp.concatenate(
        [
            jnp.sum(
                jnp.where(eye, jnp.broadcast_to(flags[s : s + 1], (own, own)), 0.0),
                axis=-1,
                keepdims=True,
            )
            for s in range(segs)
        ],
        axis=0,
    )
    for r in range(4):
        factor = lax.rsqrt(power[r] + 0.1 * level + 1e-05) * column
        for base, part in ((0, real[r]), (half, imag[r])):
            value = (part * factor).astype(jnp.bfloat16).reshape(segs, own, group)
            w_ref[:, :, base + r * group : base + (r + 1) * group] = value
    for copy in copies[2:]:
        copy.wait()


def rotate_kernel(seg_ref, w_ref, c_ref, s_ref, r_ref):
    segs, own, length = w_ref.shape
    half, part = length // 2, own // 2
    rows = c_ref.shape[0]
    first_half = seg_ref[0] == 0
    for seg in range(segs):
        w = w_ref[seg].astype(jnp.float32)
        low, high = w[:part], w[part:]
        keep = jnp.where(first_half, low, high)
        send = jnp.where(first_half, high, low)
        keep2 = jnp.concatenate([keep, keep], axis=0)
        send2 = jnp.concatenate([send, send], axis=0)
        for start in range(0, 2 * rows, 2 * own):
            pieces = []
            for row in (start, start + own):
                w2 = keep2 if row < rows else send2
                at = row % rows
                pieces.append((w2[:, :half], w2[:, half:], at))
            top, bottom = [], []
            for re, im, at in pieces:
                c, s = c_ref[at : at + own], s_ref[at : at + own]
                top.append(re * c + im * s)
                bottom.append(im * c - re * s)
            stop = start + 2 * own
            r_ref[seg, start:stop, :half] = jnp.concatenate(top, axis=0).astype(jnp.bfloat16)
            r_ref[seg, start:stop, half:] = jnp.concatenate(bottom, axis=0).astype(jnp.bfloat16)


def products(r_ref, blocks, start, rows):
    total = None
    for seg in range(r_ref.shape[0]):
        term = lax.dot_general(
            r_ref[seg, start : start + rows],
            jnp.concatenate([block[seg] for block in blocks], axis=0),
            (((1,), (1,)), ((), ())),
            preferred_element_type=jnp.float32,
        )
        total = term if total is None else total + term
    return total


def send_kernel(*refs):
    r_ref, blocks, send_ref = refs[0], refs[1:-1], refs[-1]
    rows = send_ref.shape[0]
    send_ref[...] = products(r_ref, blocks, rows, rows).astype(send_ref.dtype)


def keep_kernel(*refs):
    r_ref, blocks, keep_ref = refs[0], refs[1:-1], refs[-1]
    keep_ref[...] = products(r_ref, blocks, 0, keep_ref.shape[0])


def finish_kernel(scale, own, me_ref, keep_ref, got_ref, out_ref):
    lags, part, _ = out_ref.shape
    value = (keep_ref[...] + got_ref[...].astype(jnp.float32)) * scale
    lane = lax.broadcasted_iota(jnp.int32, value.shape, 1)
    me = me_ref[0]
    block = (lane // own) ^ me
    crossed = (block & ~6) | ((block & 2) << 1) | ((block & 4) >> 1)
    block = jnp.where(((me & 1) != 0) & (block > 7), crossed, block)
    index = block * own + lane % own
    value = jnp.take_along_axis(value, index, axis=1)
    for lag in range(lags):
        out_ref[lag] = value[lag * part : (lag + 1) * part]


CORE, SIDE, NEAR = 1, 2, 4


def gather_plan(col):
    cross = NEAR | SIDE
    held, plan = [0], []
    bit = col // 2
    while bit > NEAR:
        plan += [(m | bit, m, bit, bit) for m in held]
        held += [m | bit for m in held]
        bit //= 2
    far = held[1:]
    plan += [(m | cross, 0, m | cross, m | cross) for m in held]
    for m in held:
        a, b = (NEAR, SIDE) if m else (SIDE, NEAR)
        plan += [(m | SIDE, m, SIDE, a), (m | NEAR, m, NEAR, b)]
    mates = [0, cross] + far + [SIDE, NEAR]
    for m in far:
        mates += [m | SIDE, m | cross, m | NEAR]
    return plan + [(m | CORE, m, CORE, CORE) for m in mates]


def gather(own_block, col):
    blocks = {0: own_block}
    for block, source, even, odd in gather_plan(col):
        pairs = [(i, i ^ (odd if i & 1 else even)) for i in range(col)]
        blocks[block] = lax.ppermute(blocks[source], "col", pairs)
    order = [m ^ (6 if m & 1 and (m & 6) in (SIDE, NEAR) and m > 7 else 0) for m in range(col)]
    return [blocks[m] for m in order]


def fast_device(traces, valid):
    return fast_body(traces, valid)


def fast_body(traces, valid):
    segs, own, length = traces.shape
    col = lax.axis_size("col")
    lags, part, lanes = 2 * MAXLAG + 1, own // 2, own * col
    half = length // 2
    rows = -(-lags * part // own) * own
    me = lax.axis_index("col").astype(jnp.int32).reshape(1)
    seg_index = lax.axis_index("seg").astype(jnp.int32).reshape(1)
    scale = 1.0 / math.sqrt(segs * lax.axis_size("seg") * half)

    lag_cos, lag_sin = lag_tables(length, MAXLAG, part, rows)
    whitened, cosines, sines = pl.pallas_call(
        whiten_kernel,
        out_shape=[
            jax.ShapeDtypeStruct(traces.shape, jnp.bfloat16),
            jax.ShapeDtypeStruct(lag_cos.shape, jnp.float32),
            jax.ShapeDtypeStruct(lag_sin.shape, jnp.float32),
        ],
        in_specs=[HBM] * 4,
        out_specs=[VMEM] * 3,
        scratch_shapes=[
            pltpu.VMEM(traces.shape, traces.dtype),
            pltpu.VMEM(valid.shape, valid.dtype),
            pltpu.VMEM((length // 4, length), jnp.bfloat16),
            pltpu.VMEM((2, length // 64, half), jnp.float32),
            pltpu.SemaphoreType.DMA((4,)),
        ],
        compiler_params=grant(4),
    )(
        *[
            pltpu.with_memory_space_constraint(jnp.asarray(t), pltpu.HBM)
            for t in (traces, valid, lag_cos, lag_sin)
        ]
    )

    blocks = gather(whitened, col)

    rotated = pl.pallas_call(
        rotate_kernel,
        out_shape=jax.ShapeDtypeStruct((segs, 2 * rows, length), jnp.bfloat16),
        in_specs=[SMEM, VMEM, VMEM, VMEM],
        out_specs=VMEM,
        compiler_params=grant(8),
        cost_estimate=pl.CostEstimate(
            flops=12 * segs * rows * length,
            bytes_accessed=4 * segs * rows * length,
            transcendentals=0,
        ),
    )(seg_index, whitened, cosines, sines)

    def multiply(kernel, dtype):
        return pl.pallas_call(
            kernel,
            out_shape=jax.ShapeDtypeStruct((rows, lanes), dtype),
            in_specs=[VMEM] * (1 + len(blocks)),
            out_specs=VMEM,
            compiler_params=grant(8),
            cost_estimate=pl.CostEstimate(
                flops=2 * rows * segs * length * lanes,
                bytes_accessed=2 * (rows + lanes) * segs * length,
                transcendentals=0,
            ),
        )(*[pltpu.with_memory_space_constraint(x, pltpu.VMEM) for x in (rotated, *blocks)])

    send = multiply(send_kernel, jnp.bfloat16)
    got = lax.ppermute(send, "seg", [(0, 1), (1, 0)])
    keep = multiply(keep_kernel, jnp.float32)
    out = pl.pallas_call(
        functools.partial(finish_kernel, scale, own),
        out_shape=jax.ShapeDtypeStruct((lags, part, lanes), jnp.float32),
        in_specs=[SMEM, VMEM, VMEM],
        out_specs=VMEM,
        compiler_params=grant(2),
    )(me, keep, got)
    return out[:, None]


def on_device(traces, valid):
    fast = (
        fast_mesh(lax.axis_size("row"), lax.axis_size("col"), lax.axis_size("seg"))
        and traces.shape[1] == 8
        and traces.shape[1] * lax.axis_size("col") == 128
        and traces.shape[2] % 1024 == 0
    )
    return (fast_device if fast else general_device)(traces, valid)


def fast_mesh(row, col, seg):
    return row == 1 and seg == 2 and col >= 8 and col & (col - 1) == 0


def solution(mesh):
    placed = (P("seg", ("row", "col"), None), P("seg", ("row", "col")))
    return jax.shard_map(
        on_device,
        mesh=mesh,
        in_specs=placed,
        out_specs=P(None, None, ("col", "seg"), "row"),
        check_vma=False,
    )
```
